256 devices in a mesh: tok: 64 (over x, z, core), ch: 4 (over y).
Axes of the slice: x: 4, y: 4, z: 8, core: 2. Of those that a mesh axis runs over, the one named last changes fastest.
Arguments:
- inputs: float32 [65536, 1024], P('tok', 'ch'), may hold values from -6 to 6
- factor_one: float32 [512, 512], replicated, may hold values from -0.25 to 0.25
- twiddle: float32 [128, 512], P('tok'), may hold values from -4 to 4
- factor_two: float32 [128, 128], replicated, may hold values from -0.5 to 0.5
- w_up: bfloat16 [4, 256, 1024], P('ch', 'tok'), may hold values from -0.375 to 0.375
- w_down: bfloat16 [4, 1024, 256], P('ch', 'tok'), may hold values from -0.1875 to 0.1875
- out_cotangent: float32 [65536, 1024], P('tok', 'ch'), may hold values from -6 to 6
Outputs:
- outputs: float32 [65536, 1024], P('tok', 'ch')
- grad_inputs: float32 [65536, 1024], P('tok', 'ch')
- grad_factor_one: float32 [512, 512], replicated
- grad_factor_two: float32 [128, 128], replicated
- grad_up: float32 [4, 256, 1024], P('ch', 'tok')
- grad_down: float32 [4, 1024, 256], P('ch', 'tok')
The draws below stay inside these ranges and needn't reach their ends.
All inputs are finite; a program needn't handle non-finite values.
Results may differ from the reference program's by a relative error of at most 0.0057.
Values may be sent and summed in bfloat16 or wider, within the bound.
A program may use at most 64 MiB of HBM per device.

```python
import math
import jax
import jax.numpy as jnp
from jax import lax

D = 1024
NB = 4
M1 = 512
R = 128
L = 65536
DB = 256
FB = 1024


def level_of(rng, shape, cuts, least, high):
    loudness = 1.0
    for axis_at, shards_of in cuts:
        steps = jax.random.uniform(jax.random.fold_in(jax.random.fold_in(rng, 6), axis_at), (shards_of,), jnp.float32, least / len(cuts), high / len(cuts))
        loudness = loudness * jnp.repeat(jnp.exp(steps), shape[axis_at] // shards_of).reshape((-1,) + (1,) * (len(shape) - 1 - axis_at))
    return loudness


def gaussian(key, extent, deviation, bound, pieces=(), held_as=jnp.bfloat16):
    drawn = jax.random.normal(key, extent, jnp.float32) * deviation
    if len(pieces) > 0:
        drawn = level_of(key, extent, pieces, -0.22, 0.18) * drawn
    return jnp.clip(drawn, min=-bound, max=bound).astype(held_as)


def setup_inputs(seed: int = 0) -> dict:
    key_of = jax.random.split(jax.random.key(seed), 8)
    inputs = gaussian(key_of[0], (L, D), 1.0, 6.0, ((0, 64), (1, 4)), jnp.float32)
    factor_one = gaussian(key_of[1], (M1, M1), M1 ** -0.5, 0.25, (), jnp.float32)
    twiddle = gaussian(key_of[2], (R, M1), 1.0, 4.0, ((0, 64),), jnp.float32)
    factor_two = gaussian(key_of[3], (R, R), R ** -0.5, 0.5, (), jnp.float32)
    w_up = gaussian(key_of[4], (NB, DB, FB), DB ** -0.5, 0.375, ((0, 4), (1, 64)))
    w_down = gaussian(key_of[5], (NB, FB, DB), FB ** -0.5, 0.1875, ((0, 4), (1, 64)))
    out_cotangent = gaussian(key_of[6], (L, D), 1.0, 6.0, ((0, 64), (1, 4)), jnp.float32)
    return {"inputs": inputs, "factor_one": factor_one, "twiddle": twiddle, "factor_two": factor_two, "w_up": w_up, "w_down": w_down, "out_cotangent": out_cotangent}


inv_root_two = 1.0 / math.sqrt(2.0)
inv_root_tau = 1.0 / math.sqrt(2.0 * math.pi)

def gelu_parts(value):
    cdf = 0.5 * (1.0 + jax.scipy.special.erf(value * inv_root_two))
    return (value * cdf, cdf + value * jnp.exp(-0.5 * value * value) * inv_root_tau)

def mlp_block(items):
    normed_b, cot_b, up_w, down_w = items
    up = jnp.dot(normed_b, up_w, preferred_element_type=jnp.float32)
    active, slope = gelu_parts(up)
    hidden = active.astype(jnp.bfloat16)
    branch_out = jnp.dot(hidden, down_w, preferred_element_type=jnp.float32)
    d_hidden = jnp.dot(cot_b, down_w.T, preferred_element_type=jnp.float32)
    d_up = (d_hidden * slope).astype(jnp.bfloat16)
    d_normed = jnp.dot(d_up, up_w.T, preferred_element_type=jnp.float32)
    grad_down_b = jnp.dot(hidden.T, cot_b, preferred_element_type=jnp.float32)
    grad_up_b = jnp.dot(normed_b.T, d_up, preferred_element_type=jnp.float32)
    return (branch_out, d_normed, grad_up_b, grad_down_b)

def reference(inputs, factor_one, twiddle, factor_two, w_up, w_down, out_cotangent):
    high = lax.Precision.HIGHEST
    grid = inputs.reshape(R, M1, D)
    first = jnp.einsum('kj,ijc->ikc', factor_one, grid, precision=high)
    mid = first * twiddle[:, :, None]
    mixed = jnp.einsum('mi,ikc->mkc', factor_two, mid, precision=high).reshape(L, D)
    gate = jax.nn.sigmoid(inputs)
    branch = inputs + gate * mixed
    normed = branch.astype(jnp.bfloat16)
    cot = out_cotangent.astype(jnp.bfloat16)
    normed_blocks = normed.reshape(L, NB, DB).transpose(1, 0, 2)
    cot_blocks = cot.reshape(L, NB, DB).transpose(1, 0, 2)
    branch_out, d_normed, grad_up, grad_down = lax.map(mlp_block, (normed_blocks, cot_blocks, w_up, w_down))
    outputs = branch + branch_out.transpose(1, 0, 2).reshape(L, D)
    d_branch = out_cotangent + d_normed.transpose(1, 0, 2).reshape(L, D)
    d_mixed = d_branch * gate
    direct = d_branch * (1.0 + gate * (1.0 - gate) * mixed)
    cot_grid = d_mixed.reshape(R, M1, D)
    d_mid = jnp.einsum('mi,mkc->ikc', factor_two, cot_grid, precision=high)
    grad_factor_two = jnp.einsum('mkc,ikc->mi', cot_grid, mid, precision=high)
    d_first = d_mid * twiddle[:, :, None]
    grad_factor_one = jnp.einsum('ikc,ijc->kj', d_first, grid, precision=high)
    d_grid = jnp.einsum('kj,ikc->ijc', factor_one, d_first, precision=high)
    grad_inputs = direct + d_grid.reshape(L, D)
    return (outputs, grad_inputs, grad_factor_one, grad_factor_two, grad_up, grad_down)
```

```python
import functools
import math

import jax
import jax.numpy as jnp
from jax import lax
from jax.experimental import pallas as pl
from jax.experimental.pallas import tpu as pltpu
from jax.sharding import PartitionSpec as P

inv_root_two = 1.0 / math.sqrt(2.0)
inv_root_tau = 1.0 / math.sqrt(2.0 * math.pi)
f32 = jnp.float32
bf16 = jnp.bfloat16

A1, A2, A3, A4, WZ, WX, WC, GC, GX, GZ, TC, TZ, TX, TY, TZ2, TC2, PC, PY, PQ, PQ2, PY2, PC2 = range(22)


def gelu_parts(value):
    cdf = 0.5 * (1.0 + lax.erf(value * inv_root_two))
    return (value * cdf, cdf + value * jnp.exp(-0.5 * value * value) * inv_root_tau)


def mm(a, b):
    return jnp.dot(a, b, preferred_element_type=f32)


def mm_nt(a, b):
    return lax.dot_general(a, b, (((1,), (1,)), ((), ())), preferred_element_type=f32)


def mm_tn(a, b):
    return lax.dot_general(a, b, (((0,), (0,)), ((), ())), preferred_element_type=f32)


def split(a):
    high = a.astype(bf16)
    return high, (a - high.astype(f32)).astype(bf16)


def kernel(X, Z, Y, x_ref, f1_ref, tw_ref, f2_ref, wu_ref, wd_ref, oc_ref,
           out_ref, gx_ref, g1_ref, g2_ref, gu_ref, gd_ref,
           sa, ra, kh, kl, kth, ktl, wbuf, wup, wdn, stage, rows4, dhid, hid, dup, nrm, cot,
           gbuf, rgc, sgx, rgx, sgz, rgz, tpart, rtc, stz, rtz, rtx, rty, rt2,
           ppart, rpc, spy, rpy, spq, rpq, fin, fy, wpack, ssem, rsem):
    NQ = X * Z
    nt = 2 * NQ
    C = x_ref.shape[3]
    M = 8 * nt
    N = 16 * nt
    R = 2 * nt
    LY = M // Y
    W = min(C, 128)
    t = lax.axis_index("tok")
    y = lax.axis_index("ch")
    core = lax.rem(t, 2)
    q = lax.div(t, 2)
    z = lax.rem(q, Z)
    xx = lax.div(q, Z)
    sib = t + 1 - 2 * core
    other = 1 - core

    def tok_of(x_at, z_at):
        return (x_at * Z + z_at) * 2 + core

    def push(which, src, dst, tok, ch):
        pltpu.make_async_remote_copy(
            src_ref=src, dst_ref=dst, send_sem=ssem.at[which], recv_sem=rsem.at[which],
            device_id=(tok, ch), device_id_type=pl.DeviceIdType.MESH,
        ).start()

    def arrive(which, view):
        pltpu.make_async_copy(view, view, rsem.at[which]).wait()

    def sent(which, view):
        pltpu.make_async_copy(view, view, ssem.at[which]).wait()

    def each(count, body):
        def step(d, carry):
            body(d)
            return carry
        lax.fori_loop(1, count, step, 0)

    barrier = pltpu.get_barrier_semaphore()

    def greet_tok(d):
        pl.semaphore_signal(barrier, inc=1, device_id=(lax.rem(t + d, nt), y), device_id_type=pl.DeviceIdType.MESH)

    def greet_ch(d):
        pl.semaphore_signal(barrier, inc=1, device_id=(t, lax.rem(y + d, Y)), device_id_type=pl.DeviceIdType.MESH)

    each(nt, greet_tok)
    each(Y, greet_ch)

    f1h, f1l = split(f1_ref[...])
    eye = lax.broadcasted_iota(jnp.int32, (M, M), 0) == lax.broadcasted_iota(jnp.int32, (M, M), 1)

    def tw_col(i):
        return jnp.sum(jnp.where(eye, tw_ref[i : i + 1, :], 0.0), axis=1, keepdims=True)

    def pair(a, b):
        n = a.shape[0]
        return jnp.concatenate([a[:, None], b[:, None]], axis=1).reshape(n, 16, C)

    mids = []
    for i in range(2):
        xh, xl = split(x_ref[i].reshape(M, C))
        first = mm(f1h, xh) + mm(f1h, xl) + mm(f1l, xh)
        mids.append((first * tw_col(i)).reshape(nt, 8, C))
    sa[0] = pair(mids[0], mids[1]).astype(bf16)
    ra[0, t] = sa[0, t]

    wpack[...] = jnp.concatenate(
        [wd_ref[...].astype(f32)] + [wu_ref[:, fq * C : (fq + 1) * C].astype(f32) for fq in range(4)], axis=0)
    wbuf[core, xx, z] = wpack[...].astype(bf16)

    pl.semaphore_wait(barrier, nt - 1 + Y - 1)

    def a2a(phase):
        def one(d):
            peer = lax.rem(t + d, nt)
            push(phase, sa.at[phase, peer], ra.at[phase, t], peer, y)
        each(nt, one)

    def a2a_arrive(phase):
        arrive(phase, ra.at[phase, pl.ds(0, nt - 1)])

    a2a(A1)
    each(Z, lambda d: push(WZ, wbuf.at[core, xx, z], wbuf.at[core, xx, z], tok_of(xx, lax.rem(z + d, Z)), y))

    f2h, f2l = split(f2_ref[...])
    f2t = f2_ref[...].T
    f2th, f2tl = split(f2t)
    band = min(N // 2, 128)
    spread = (lax.broadcasted_iota(jnp.int32, (N, R), 0) >> 3) == lax.broadcasted_iota(jnp.int32, (N, R), 1)
    spread = jnp.where(spread, 1.0, 0.0).astype(bf16)

    def build(src, dst):
        def step(b, carry):
            r0 = pl.multiple_of(b * band, band)
            rows = (lax.broadcasted_iota(jnp.int32, (band, R), 0) + r0) >> 3
            pick = jnp.where(rows == lax.broadcasted_iota(jnp.int32, (band, R), 1), 1.0, 0.0).astype(bf16)
            part = mm_nt(mm(pick, src).astype(bf16), spread)
            same = ((lax.broadcasted_iota(jnp.int32, (band, N), 0) & 7)
                    == (lax.broadcasted_iota(jnp.int32, (band, N), 1) & 7))
            dst[pl.ds(r0, band), :] = jnp.where(same, part, 0.0).astype(bf16)
            return carry
        lax.fori_loop(0, N // band, step, 0)

    build(f2h, kh)
    build(f2l, kl)

    arrive(WZ, wbuf.at[core, xx, pl.ds(0, Z - 1)])
    each(X, lambda d: push(WX, wbuf.at[core, xx], wbuf.at[core, xx], tok_of(lax.rem(xx + d, X), z), y))

    a2a_arrive(A1)
    mid = ra[0].reshape(N, C)
    sa[1] = (mm(kh[...], mid) + mm(kl[...], mid)).astype(bf16).reshape(nt, 16, C)
    ra[1, t] = sa[1, t]
    a2a(A2)

    arrive(WX, wbuf.at[core, pl.ds(0, X - 1)])
    push(WC, wbuf.at[core], wbuf.at[core], sib, y)
    build(f2th, kth)
    build(f2tl, ktl)
    arrive(WC, wbuf.at[other])

    for c in range(2):
        wdn[:, c] = wbuf[c, :, :, 0:16].reshape(NQ, 16, C)
    up_rows = [wbuf[c, :, :, 16:32].astype(f32).reshape(NQ, 1, 16, C) for c in range(2)]
    up_rows = jnp.concatenate(up_rows, axis=1).reshape(N, C)
    for h in range(C // W):
        rows4[h] = up_rows[:, h * W : (h + 1) * W]
    for fq in range(4):
        for h in range(C // W):
            for r in range(4):
                stage[pl.ds(r, nt, stride=4), :] = rows4[h, pl.ds(4 * fq + r, nt, stride=16), :]
            wup[:, fq * C + h * W : fq * C + (h + 1) * W] = stage[...].astype(bf16)

    nb = max(1, nt // 4)
    tiles = nt // nb

    def tokens(ref, s0):
        return pair(ref[0, pl.ds(s0, nb)], ref[1, pl.ds(s0, nb)]).reshape(nb * 16, C)

    def put(ref, s0, value):
        value = value.reshape(nb, 2, 8, C)
        ref[0, pl.ds(s0, nb)] = value[:, 0]
        ref[1, pl.ds(s0, nb)] = value[:, 1]

    down = wdn[...].reshape(N, C)

    def pre(j, carry):
        s0 = pl.multiple_of(j * nb, nb)
        r0 = pl.multiple_of(j * nb * 16, nb * 16)
        c16 = tokens(oc_ref, s0).astype(bf16)
        cot[pl.ds(r0, nb * 16), :] = c16
        dhid[pl.ds(r0, nb * 16), :] = mm_nt(c16, wdn[...].reshape(N, C))
        return carry

    lax.fori_loop(0, tiles, pre, 0)

    a2a_arrive(A2)

    def mlp(j, carry):
        tile = lax.rem(lax.div(t, nb) + j, tiles)
        s0 = pl.multiple_of(tile * nb, nb)
        r0 = pl.multiple_of(tile * nb * 16, nb * 16)
        rows = pl.ds(r0, nb * 16)
        mixed = ra[1, pl.ds(s0, nb)].reshape(nb * 16, C).astype(f32)
        inp = tokens(x_ref, s0)
        gate = jax.nn.sigmoid(inp)
        branch = inp + gate * mixed
        normed = branch.astype(bf16)
        nrm[rows, :] = normed
        up = mm(normed, wup[...])
        active, slope = gelu_parts(up)
        hidden = active.astype(bf16)
        hid[rows, :] = hidden
        put(out_ref, s0, branch + mm(hidden, wdn[...].reshape(N, C)))
        d_up = (dhid[rows, :] * slope).astype(bf16)
        dup[rows, :] = d_up
        d_branch = tokens(oc_ref, s0) + mm_nt(d_up, wup[...])
        sa[2, pl.ds(s0, nb)] = (d_branch * gate).astype(bf16).reshape(nb, 16, C)
        put(gx_ref, s0, d_branch * (1.0 + gate * (1.0 - gate) * mixed))

        def one(b, inner):
            peer = s0 + lax.rem(t + b, nb)

            @pl.when(peer != t)
            def _():
                push(A3, sa.at[2, peer], ra.at[2, t], peer, y)

            return inner

        lax.fori_loop(0, nb, one, 0)
        return carry

    lax.fori_loop(0, tiles, mlp, 0)
    ra[2, t] = sa[2, t]

    gd_part = mm_tn(hid[...], cot[...]).reshape(NQ, 2, 16, C)
    for c in range(2):
        gbuf[c, :, 0:16] = gd_part[:, c]
    for fq in range(4):
        gu_part = mm_tn(nrm[...], dup[:, fq * C : (fq + 1) * C])
        for h in range(C // W):
            stage[...] = gu_part[:, h * W : (h + 1) * W]
            for r in range(4):
                rows4[h, pl.ds(4 * fq + r, nt, stride=16), :] = stage[pl.ds(r, nt, stride=4), :]
    for c in range(2):
        for h in range(C // W):
            gbuf[c, :, 16:32, h * W : (h + 1) * W] = rows4[h].reshape(NQ, 2, 16, W)[:, c]
    push(GC, gbuf.at[other], rgc, sib, y)

    a2a_arrive(A3)
    grad = ra[2].reshape(N, C)
    sa[3] = (mm(kth[...], grad) + mm(ktl[...], grad)).astype(bf16).reshape(nt, 16, C)
    ra[3, t] = sa[3, t]
    a2a(A4)

    arrive(GC, rgc)
    sgx[...] = (gbuf[core] + rgc[...]).astype(bf16).reshape(X, Z, 32, C)

    def send_gx(d):
        peer = lax.rem(xx + d, X)
        push(GX, sgx.at[peer], rgx.at[xx], tok_of(peer, z), y)

    each(X, send_gx)

    def two(b, carry):
        r0 = pl.multiple_of(b * band, band)
        prod = mm_nt(ra[2, pl.ds(b * (band // 16), band // 16)].reshape(band, C), ra[0].reshape(N, C))
        same = ((lax.broadcasted_iota(jnp.int32, (band, N), 0) & 7)
                == (lax.broadcasted_iota(jnp.int32, (band, N), 1) & 7))
        ph, pw = split(jnp.where(same, prod, 0.0))
        tpart[b] = (mm(ph, spread) + mm(pw, spread)).reshape(band // 8, 8, R).sum(axis=1)
        return carry

    lax.fori_loop(0, N // band, two, 0)
    half = tpart.shape[0] // 2
    push(TC, tpart.at[pl.ds(other * half, half)], rtc, sib, y)

    arrive(GX, rgx.at[pl.ds(0, X - 1)])
    rgx[xx] = jnp.zeros((Z, 32, C), bf16)
    zrows = pl.ds(xx * Z, Z)
    own_gz = gbuf[core, zrows] + rgc[zrows]
    for s in range(X):
        own_gz = own_gz + rgx[s].astype(f32)
    gbuf[core, zrows] = own_gz
    sgz[...] = own_gz.astype(bf16)

    def send_gz(d):
        peer = lax.rem(z + d, Z)
        push(GZ, sgz.at[peer], rgz.at[z], tok_of(xx, peer), y)

    each(Z, send_gz)

    arrive(TC, rtc)
    stz[...] = (tpart[pl.ds(core * half, half)] + rtc[...]).reshape(Z, nt // Z, R)

    def send_tz(d):
        peer = lax.rem(z + d, Z)
        push(TZ, stz.at[peer], rtz.at[z], tok_of(xx, peer), y)

    each(Z, send_tz)

    arrive(GZ, rgz.at[pl.ds(0, Z - 1)])
    rgz[z] = jnp.zeros((32, C), bf16)
    wpack[...] = gbuf[core, xx * Z + z] + rgz[...].astype(f32).sum(axis=0)
    gd_ref[...] = wpack[0:16, :]
    for fq in range(4):
        gu_ref[:, fq * C : (fq + 1) * C] = wpack[16 + 4 * fq : 20 + 4 * fq, :]

    arrive(TZ, rtz.at[pl.ds(0, Z - 1)])
    rtz[z] = stz[z]
    rtx[xx] = rtz[...].sum(axis=0)
    each(X, lambda d: push(TX, rtx.at[xx], rtx.at[xx], tok_of(lax.rem(xx + d, X), z), y))
    arrive(TX, rtx.at[pl.ds(0, X - 1)])
    rty[y] = rtx[...].sum(axis=0)
    each(Y, lambda d: push(TY, rty.at[y], rty.at[y], t, lax.rem(y + d, Y)))
    arrive(TY, rty.at[pl.ds(0, Y - 1)])
    rt2[core, z] = rty[...].sum(axis=0)
    each(Z, lambda d: push(TZ2, rt2.at[core, z], rt2.at[core, z], tok_of(xx, lax.rem(z + d, Z)), y))

    a2a_arrive(A4)
    d_mid = ra[3].astype(f32).reshape(nt, 2, 8, C)
    d_first = [(d_mid[:, i].reshape(M, C) * tw_col(i)).astype(bf16) for i in range(2)]
    one = mm_nt(d_first[0], x_ref[0].reshape(M, C).astype(bf16)) + mm_nt(d_first[1], x_ref[1].reshape(M, C).astype(bf16))
    one = one.reshape(NQ, 2, 8, M)
    for c in range(2):
        for v in range(Y):
            ppart[c, v] = one[:, c, :, v * LY : (v + 1) * LY]
    push(PC, ppart.at[other], rpc, sib, y)

    arrive(TZ2, rt2.at[core, pl.ds(0, Z - 1)])
    push(TC2, rt2.at[core], rt2.at[core], sib, y)

    f1t = f1_ref[...].T.astype(bf16)
    for i in range(2):
        gx_ref[i] = gx_ref[i] + mm(f1t, d_first[i]).reshape(nt, 8, C)

    arrive(PC, rpc)
    spy[...] = (ppart[core] + rpc[...]).astype(bf16).reshape(Y, NQ * 8, LY)

    def send_py(d):
        peer = lax.rem(y + d, Y)
        push(PY, spy.at[peer], rpy.at[y], t, peer)

    each(Y, send_py)
    arrive(TC2, rt2.at[other])
    g2_ref[...] = rt2[...].reshape(R, R)
    arrive(PY, rpy.at[pl.ds(0, Y - 1)])
    rpy[y] = jnp.zeros((NQ * 8, LY), bf16)
    total = (ppart[core, y] + rpc[y]).reshape(NQ * 8, LY)
    for s in range(Y):
        total = total + rpy[s].astype(f32)
    spq[...] = total.reshape(NQ, 8, LY)

    def send_pq(d):
        peer = lax.rem(q + d, NQ)
        push(PQ, spq.at[peer], rpq.at[q], 2 * peer + core, y)

    each(NQ, send_pq)
    arrive(PQ, rpq.at[pl.ds(0, NQ - 1)])
    rpq[q] = spq[q]
    fin[q] = rpq[...].sum(axis=0).astype(bf16).astype(f32)
    each(NQ, lambda d: push(PQ2, fin.at[q], fin.at[q], 2 * lax.rem(q + d, NQ) + core, y))
    arrive(PQ2, fin.at[pl.ds(0, NQ - 1)])
    fy[core, y] = fin[...].reshape(NQ * 8, LY).astype(bf16)
    each(Y, lambda d: push(PY2, fy.at[core, y], fy.at[core, y], t, lax.rem(y + d, Y)))
    arrive(PY2, fy.at[core, pl.ds(0, Y - 1)])
    push(PC2, fy.at[core], fy.at[core], sib, y)
    arrive(PC2, fy.at[other])
    for c in range(2):
        for v in range(Y):
            g1_ref[:, c, :, v * LY : (v + 1) * LY] = fy[c, v].astype(f32).reshape(NQ, 8, LY)

    for phase in (A1, A2, A3, A4):
        sent(phase, sa.at[phase, pl.ds(0, nt - 1)])
    sent(WZ, wbuf.at[0, 0, pl.ds(0, Z - 1)])
    sent(WX, wbuf.at[0, pl.ds(0, X - 1)])
    sent(WC, wbuf.at[0])
    sent(GC, rgc)
    sent(GX, sgx.at[pl.ds(0, X - 1)])
    sent(GZ, sgz.at[pl.ds(0, Z - 1)])
    sent(TC, rtc)
    sent(TZ, stz.at[pl.ds(0, Z - 1)])
    sent(TX, rtx.at[pl.ds(0, X - 1)])
    sent(TY, rty.at[pl.ds(0, Y - 1)])
    sent(TZ2, rt2.at[0, pl.ds(0, Z - 1)])
    sent(TC2, rt2.at[0])
    sent(PC, rpc)
    sent(PY, spy.at[pl.ds(0, Y - 1)])
    sent(PQ, spq.at[pl.ds(0, NQ - 1)])
    sent(PQ2, fin.at[pl.ds(0, NQ - 1)])
    sent(PY2, fy.at[0, pl.ds(0, Y - 1)])
    sent(PC2, fy.at[0])


def local(X, Z, Y, inputs, factor_one, twiddle, factor_two, w_up, w_down, out_cotangent):
    NQ = X * Z
    nt = 2 * NQ
    C = inputs.shape[1]
    M = 8 * nt
    N = 16 * nt
    R = 2 * nt
    LY = M // Y
    W = min(C, 128)
    band = min(N // 2, 128)
    V = pltpu.VMEM
    scratch = [
        V((4, nt, 16, C), bf16), V((4, nt, 16, C), bf16),
        V((N, N), bf16), V((N, N), bf16), V((N, N), bf16), V((N, N), bf16),
        V((2, X, Z, 32, C), bf16), V((C, 4 * C), bf16), V((NQ, 2, 16, C), bf16),
        V((C, W), f32), V((C // W, N, W), f32),
        V((N, 4 * C), f32), V((N, 4 * C), bf16), V((N, 4 * C), bf16), V((N, C), bf16), V((N, C), bf16),
        V((2, NQ, 32, C), f32), V((NQ, 32, C), f32),
        V((X, Z, 32, C), bf16), V((X, Z, 32, C), bf16), V((Z, 32, C), bf16), V((Z, 32, C), bf16),
        V((N // band, band // 8, R), f32), V((N // band // 2, band // 8, R), f32),
        V((Z, nt // Z, R), f32), V((Z, nt // Z, R), f32), V((X, nt // Z, R), f32), V((Y, nt // Z, R), f32),
        V((2, Z, nt // Z, R), f32),
        V((2, Y, NQ, 8, LY), f32), V((Y, NQ, 8, LY), f32),
        V((Y, NQ * 8, LY), bf16), V((Y, NQ * 8, LY), bf16),
        V((NQ, 8, LY), f32), V((NQ, 8, LY), f32), V((NQ, 8, LY), f32), V((2, Y, NQ * 8, LY), bf16),
        V((32, C), f32),
        pltpu.SemaphoreType.DMA((22,)), pltpu.SemaphoreType.DMA((22,)),
    ]
    shapes = [
        ((2, nt, 8, C), f32), ((2, nt, 8, C), f32), ((NQ, 2, 8, M), f32), ((R, R), f32),
        ((4, 4 * C), f32), ((16, C), f32),
    ]
    vm = pl.BlockSpec(memory_space=pltpu.VMEM)
    out, gx, g1, g2, gu, gd = pl.pallas_call(
        functools.partial(kernel, X, Z, Y),
        out_shape=[jax.ShapeDtypeStruct(*s) for s in shapes],
        in_specs=[vm] * 7,
        out_specs=[vm] * 6,
        scratch_shapes=scratch,
        compiler_params=pltpu.CompilerParams(
            collective_id=0, has_side_effects=True, vmem_limit_bytes=60 * 1024 * 1024),
        name="monarch",
    )(
        inputs.reshape(2, nt, 8, C), factor_one, twiddle, factor_two,
        w_up[0], w_down[0], out_cotangent.reshape(2, nt, 8, C),
    )
    return (out.reshape(2 * M, C), gx.reshape(2 * M, C), g1.reshape(M, M), g2, gu[None], gd[None])


def solution(mesh):
    nt = mesh.shape["tok"]
    Y = mesh.shape["ch"]
    X = 4 if nt == 64 else 2
    in_specs = (
        P("tok", "ch"),
        P(),
        P("tok", None),
        P(),
        P("ch", "tok", None),
        P("ch", "tok", None),
        P("tok", "ch"),
    )
    out_specs = (
        P("tok", "ch"),
        P("tok", "ch"),
        P(),
        P(),
        P("ch", "tok", None),
        P("ch", "tok", None),
    )
    return jax.shard_map(
        functools.partial(local, X, nt // 2 // X, Y), mesh=mesh, in_specs=in_specs, out_specs=out_specs, check_vma=False)
```

```python
import functools
import math

import jax
import jax.numpy as jnp
from jax import lax
from jax.experimental import pallas as pl
from jax.experimental.pallas import tpu as pltpu
from jax.sharding import PartitionSpec as P

inv_root_two = 1.0 / math.sqrt(2.0)
inv_root_tau = 1.0 / math.sqrt(2.0 * math.pi)
f32 = jnp.float32
bf16 = jnp.bfloat16

(A1, A2, A2B, A3, A4, A4B, WZ, WX, WC, GC, GX, GZ, TC, TZ, TX, TY, TZ2, TC2, PC, PY, PQ, PQ2, PY2, PC2) = range(24)
NEX = 24
LX, LF1, LOC, LTW, LF2, LWU, LWD = range(7)


def gelu_parts(value):
    cdf = 0.5 * (1.0 + lax.erf(value * inv_root_two))
    return (value * cdf, cdf + value * jnp.exp(-0.5 * value * value) * inv_root_tau)


def mm(a, b):
    return jnp.dot(a, b, preferred_element_type=f32)


def mm_nt(a, b):
    return lax.dot_general(a, b, (((1,), (1,)), ((), ())), preferred_element_type=f32)


def mm_tn(a, b):
    return lax.dot_general(a, b, (((0,), (0,)), ((), ())), preferred_element_type=f32)


def split(a):
    high = a.astype(bf16)
    return high, (a - high.astype(f32)).astype(bf16)


def kernel(X, Z, Y, x_in, f1_in, tw_in, f2_in, wu_in, wd_in, oc_in,
           out_ref, gx_ref, fy, g2_ref, gu_ref, gd_ref,
           xv, f1v, ocv, tw_ref, f2v, wu_ref, wd_ref,
           sa, ra, kh, kth, ktl, f1t, xb, twc, wbuf, wup, wdn, stage, rows4, dhid, hid, dup, nrm, cot, df,
           gbuf, rgc, sgx, rgx, sgz, rgz, tsum, tpart, rtc, stz, rtz, rtx, rty, rt2,
           ppart, rpc, spy, rpy, spq, rpq, fin, wpack, ssem, rsem, lsem):
    NQ = X * Z
    nt = 2 * NQ
    C = xv.shape[4]
    M = 8 * nt
    H = 8 * NQ
    N = 16 * nt
    R = 2 * nt
    LY = M // Y
    W = min(C, 128)
    lgq = NQ.bit_length() - 1
    t = lax.axis_index("tok")
    y = lax.axis_index("ch")
    core = lax.rem(t, 2)
    q = lax.div(t, 2)
    z = lax.rem(q, Z)
    xx = lax.div(q, Z)
    sib = t + 1 - 2 * core
    other = 1 - core
    me = core * NQ + q

    def tok_of(x_at, z_at):
        return (x_at * Z + z_at) * 2 + core

    def push(which, src, dst, tok, ch):
        pltpu.make_async_remote_copy(
            src_ref=src, dst_ref=dst, send_sem=ssem.at[which], recv_sem=rsem.at[which],
            device_id=(tok, ch), device_id_type=pl.DeviceIdType.MESH,
        ).start()

    def arrive(which, view):
        pltpu.make_async_copy(view, view, rsem.at[which]).wait()

    def sent(which, view):
        pltpu.make_async_copy(view, view, ssem.at[which]).wait()

    def each(count, body, start=1):
        def step(d, carry):
            body(d)
            return carry
        lax.fori_loop(start, count, step, 0)

    barrier = pltpu.get_barrier_semaphore()

    def greet_tok(d):
        pl.semaphore_signal(barrier, inc=1, device_id=(lax.rem(t + d, nt), y), device_id_type=pl.DeviceIdType.MESH)

    def greet_ch(d):
        pl.semaphore_signal(barrier, inc=1, device_id=(t, lax.rem(y + d, Y)), device_id_type=pl.DeviceIdType.MESH)

    each(nt, greet_tok)
    each(Y, greet_ch)
    loads = {}
    for which, src, dst in ((LF1, f1_in, f1v), (LX, x_in, xv), (LTW, tw_in, tw_ref), (LWU, wu_in, wu_ref),
                            (LWD, wd_in, wd_ref), (LF2, f2_in, f2v), (LOC, oc_in, ocv)):
        loads[which] = pltpu.make_async_copy(src, dst, lsem.at[which])
        loads[which].start()

    loads[LF1].wait()
    f1h, f1l = split(f1v[...])
    loads[LTW].wait()
    eye = lax.broadcasted_iota(jnp.int32, (M, M), 0) == lax.broadcasted_iota(jnp.int32, (M, M), 1)
    for i in range(2):
        col = jnp.sum(jnp.where(eye, tw_ref[i : i + 1, :], 0.0), axis=1, keepdims=True)
        twc[i] = col.reshape(NQ, 2, 8, 1)

    def pair(a, b):
        n = a.shape[0]
        return jnp.concatenate([a[:, None], b[:, None]], axis=1).reshape(n, 16, C)

    loads[LX].wait()
    mids = []
    for i in range(2):
        xh, xl = split(xv[i].reshape(M, C))
        xb[i] = xh
        first = mm(f1h, xh) + mm(f1h, xl) + mm(f1l, xh)
        mids.append(first.reshape(NQ, 2, 8, C) * twc[i])
    for c in range(2):
        sa[0, c * NQ : (c + 1) * NQ] = pair(mids[0][:, c], mids[1][:, c]).astype(bf16)
    ra[0, me] = sa[0, me]

    loads[LWU].wait()
    loads[LWD].wait()
    wpack[...] = jnp.concatenate(
        [wd_ref[...].astype(f32)] + [wu_ref[:, fq * C : (fq + 1) * C].astype(f32) for fq in range(4)], axis=0)
    wbuf[core, xx, z] = wpack[...].astype(bf16)

    pl.semaphore_wait(barrier, nt - 1 + Y - 1)

    def a2a(phase, which):
        for c in range(2):
            def one(d):
                peer = lax.rem(q + d, NQ)

                @pl.when((peer != q) | (core != c))
                def _():
                    push(which, sa.at[phase, c * NQ + peer], ra.at[phase, me], 2 * peer + c, y)

            each(NQ, one, 0)

    def from_core(which, phase, c):
        @pl.when(core == c)
        def _():
            arrive(which, ra.at[phase, pl.ds(0, NQ - 1)])

        @pl.when(core != c)
        def _():
            arrive(which, ra.at[phase, pl.ds(0, NQ)])

    def from_all(which, phase):
        arrive(which, ra.at[phase, pl.ds(0, nt - 1)])

    a2a(0, A1)
    each(Z, lambda d: push(WZ, wbuf.at[core, xx, z], wbuf.at[core, xx, z], tok_of(xx, lax.rem(z + d, Z)), y))

    loads[LF2].wait()
    f2h = f2v[...].astype(bf16)
    f2th, f2tl = split(f2v[...].T)
    band = min(N // 2, 128)

    def row_of(n):
        return 4 * ((n >> 4) & (NQ - 1)) + 2 * (n >> (4 + lgq)) + ((n >> 3) & 1)

    spread = row_of(lax.broadcasted_iota(jnp.int32, (N, R), 0)) == lax.broadcasted_iota(jnp.int32, (N, R), 1)
    spread = jnp.where(spread, 1.0, 0.0).astype(bf16)
    same = ((lax.broadcasted_iota(jnp.int32, (band, N), 0) & 7) == (lax.broadcasted_iota(jnp.int32, (band, N), 1) & 7))

    def picked(r0):
        rows = row_of(lax.broadcasted_iota(jnp.int32, (band, R), 0) + r0)
        return jnp.where(rows == lax.broadcasted_iota(jnp.int32, (band, R), 1), 1.0, 0.0).astype(bf16)

    def build(src, dst):
        def step(b, carry):
            r0 = pl.multiple_of(b * band, band)
            part = mm_nt(mm(picked(r0), src).astype(bf16), spread)
            dst[pl.ds(r0, band), :] = jnp.where(same, part, 0.0).astype(bf16)
            return carry
        lax.fori_loop(0, N // band, step, 0)

    build(f2h, kh)

    arrive(WZ, wbuf.at[core, xx, pl.ds(0, Z - 1)])
    each(X, lambda d: push(WX, wbuf.at[core, xx], wbuf.at[core, xx], tok_of(lax.rem(xx + d, X), z), y))

    from_all(A1, 0)
    sa[1] = mm(kh[...], ra[0].reshape(N, C)).astype(bf16).reshape(nt, 16, C)
    ra[1, me] = sa[1, me]
    a2a(1, A2 + core)

    arrive(WX, wbuf.at[core, pl.ds(0, X - 1)])
    push(WC, wbuf.at[core], wbuf.at[core], sib, y)
    build(f2th, kth)
    build(f2tl, ktl)
    for c in range(2):
        f1t[c] = f1v[...].reshape(NQ, 2, 8, M)[:, c].reshape(H, M).T.astype(bf16)
    arrive(WC, wbuf.at[other])

    for c in range(2):
        wdn[:, c] = wbuf[c, :, :, 0:16].reshape(NQ, 16, C)
    up_rows = [wbuf[c, :, :, 16:32].astype(f32).reshape(NQ, 1, 16, C) for c in range(2)]
    up_rows = jnp.concatenate(up_rows, axis=1).reshape(N, C)
    for h in range(C // W):
        rows4[h] = up_rows[:, h * W : (h + 1) * W]
    for fq in range(4):
        for h in range(C // W):
            for r in range(4):
                stage[pl.ds(r, nt, stride=4), :] = rows4[h, pl.ds(4 * fq + r, nt, stride=16), :]
            wup[:, fq * C + h * W : fq * C + (h + 1) * W] = stage[...].astype(bf16)

    nb = max(1, NQ // 2)
    tiles = NQ // nb
    TB = nb * 16

    def tokens(ref, c, q0):
        return pair(ref[0, pl.ds(q0, nb), c], ref[1, pl.ds(q0, nb), c]).reshape(TB, C)

    def put(ref, c, q0, value):
        value = value.reshape(nb, 2, 8, C)
        ref[0, pl.ds(q0, nb), c] = value[:, 0]
        ref[1, pl.ds(q0, nb), c] = value[:, 1]

    def places(c, j):
        q0 = pl.multiple_of(j * nb, nb)
        return q0, pl.ds(pl.multiple_of(c * H * 2 + j * TB, TB), TB)

    loads[LOC].wait()
    for c in range(2):
        def pre(j, carry):
            q0, rows = places(c, j)
            c16 = tokens(ocv, c, q0).astype(bf16)
            cot[rows, :] = c16
            dhid[rows, :] = mm_nt(c16, wdn[...].reshape(N, C))
            return carry

        lax.fori_loop(0, tiles, pre, 0)

    for c in range(2):
        from_core(A2 + c, 1, c)

        def mlp(j, carry):
            tile = lax.rem(lax.div(q, nb) + j, tiles)
            q0, rows = places(c, tile)
            mixed = ra[1, pl.ds(c * NQ + q0, nb)].reshape(TB, C).astype(f32)
            inp = tokens(xv, c, q0)
            gate = jax.nn.sigmoid(inp)
            branch = inp + gate * mixed
            put(out_ref, c, q0, branch)
            normed = branch.astype(bf16)
            nrm[rows, :] = normed
            up = mm(normed, wup[...])
            active, slope = gelu_parts(up)
            hid[rows, :] = active.astype(bf16)
            d_up = (dhid[rows, :] * slope).astype(bf16)
            dup[rows, :] = d_up
            d_branch = tokens(ocv, c, q0) + mm_nt(d_up, wup[...])
            sa[2, pl.ds(c * NQ + q0, nb)] = (d_branch * gate).astype(bf16).reshape(nb, 16, C)

            def one(b, inner):
                peer = q0 + lax.rem(q + b, nb)

                @pl.when((peer != q) | (core != c))
                def _():
                    push(A3, sa.at[2, c * NQ + peer], ra.at[2, me], 2 * peer + c, y)

                return inner

            lax.fori_loop(0, nb, one, 0)
            put(gx_ref, c, q0, d_branch * (1.0 + gate * (1.0 - gate) * mixed))
            return carry

        lax.fori_loop(0, tiles, mlp, 0)
    ra[2, me] = sa[2, me]

    from_all(A3, 2)
    grad = ra[2].reshape(N, C)
    sa[3] = (mm(kth[...], grad) + mm(ktl[...], grad)).astype(bf16).reshape(nt, 16, C)
    ra[3, me] = sa[3, me]
    a2a(3, A4 + core)

    gd_part = mm_tn(hid[...], cot[...]).reshape(NQ, 2, 16, C)
    for c in range(2):
        gbuf[c, :, 0:16] = gd_part[:, c]
    for fq in range(4):
        gu_part = mm_tn(nrm[...], dup[:, fq * C : (fq + 1) * C])
        for h in range(C // W):
            stage[...] = gu_part[:, h * W : (h + 1) * W]
            for r in range(4):
                rows4[h, pl.ds(4 * fq + r, nt, stride=16), :] = stage[pl.ds(r, nt, stride=4), :]
    for c in range(2):
        for h in range(C // W):
            gbuf[c, :, 16:32, h * W : (h + 1) * W] = rows4[h].reshape(NQ, 2, 16, W)[:, c]
    push(GC, gbuf.at[other], rgc, sib, y)

    tsum[...] = jnp.zeros((R, R), f32)

    def two(b, carry):
        r0 = pl.multiple_of(b * band, band)
        blocks = ra[2, pl.ds(b * (band // 16), band // 16)]
        prod = mm_nt(blocks.reshape(band, C), ra[0].reshape(N, C))
        ph, pw = split(jnp.where(same, prod, 0.0))
        ph, pw = split(mm(ph, spread) + mm(pw, spread))
        tsum[...] += mm_tn(picked(r0), ph) + mm_tn(picked(r0), pw)
        return carry

    lax.fori_loop(0, N // band, two, 0)
    tpart[...] = tsum[...].reshape(2, nt, R)
    push(TC, tpart.at[other], rtc, sib, y)

    arrive(GC, rgc)
    sgx[...] = (gbuf[core] + rgc[...]).astype(bf16).reshape(X, Z, 32, C)

    def send_gx(d):
        peer = lax.rem(xx + d, X)
        push(GX, sgx.at[peer], rgx.at[xx], tok_of(peer, z), y)

    each(X, send_gx)

    arrive(TC, rtc)
    stz[...] = (tpart[core] + rtc[...]).reshape(Z, nt // Z, R)

    def send_tz(d):
        peer = lax.rem(z + d, Z)
        push(TZ, stz.at[peer], rtz.at[z], tok_of(xx, peer), y)

    each(Z, send_tz)

    for c in range(2):
        def finish(j, carry):
            q0, rows = places(c, j)
            put(out_ref, c, q0, tokens(out_ref, c, q0) + mm(hid[rows, :], wdn[...].reshape(N, C)))
            return carry

        lax.fori_loop(0, tiles, finish, 0)

    arrive(GX, rgx.at[pl.ds(0, X - 1)])
    rgx[xx] = jnp.zeros((Z, 32, C), bf16)
    zrows = pl.ds(xx * Z, Z)
    own_gz = gbuf[core, zrows] + rgc[zrows]
    for s in range(X):
        own_gz = own_gz + rgx[s].astype(f32)
    gbuf[core, zrows] = own_gz
    sgz[...] = own_gz.astype(bf16)

    def send_gz(d):
        peer = lax.rem(z + d, Z)
        push(GZ, sgz.at[peer], rgz.at[z], tok_of(xx, peer), y)

    each(Z, send_gz)

    arrive(TZ, rtz.at[pl.ds(0, Z - 1)])
    rtz[z] = stz[z]
    rtx[xx] = rtz[...].sum(axis=0)
    each(X, lambda d: push(TX, rtx.at[xx], rtx.at[xx], tok_of(lax.rem(xx + d, X), z), y))

    for c in range(2):
        from_core(A4 + c, 3, c)
        d_mid = ra[3, c * NQ : (c + 1) * NQ].astype(f32).reshape(NQ, 2, 8, C)
        one = None
        for i in range(2):
            d_first = (d_mid[:, i] * twc[i, :, c]).reshape(H, C).astype(bf16)
            df[c, i] = d_first
            part = mm_nt(d_first, xb[i])
            one = part if one is None else one + part
        one = one.reshape(NQ, 8, M)
        for v in range(Y):
            ppart[c, v] = one[:, :, v * LY : (v + 1) * LY]

        @pl.when(core != c)
        def _():
            push(PC, ppart.at[c], rpc, sib, y)

    arrive(PC, rpc)
    spy[...] = (ppart[core] + rpc[...]).astype(bf16).reshape(Y, NQ * 8, LY)

    def send_py(d):
        peer = lax.rem(y + d, Y)
        push(PY, spy.at[peer], rpy.at[y], t, peer)

    each(Y, send_py)

    arrive(TX, rtx.at[pl.ds(0, X - 1)])
    rty[y] = rtx[...].sum(axis=0)
    each(Y, lambda d: push(TY, rty.at[y], rty.at[y], t, lax.rem(y + d, Y)))

    arrive(GZ, rgz.at[pl.ds(0, Z - 1)])
    rgz[z] = jnp.zeros((32, C), bf16)
    wpack[...] = gbuf[core, xx * Z + z] + rgz[...].astype(f32).sum(axis=0)
    gd_ref[...] = wpack[0:16, :]
    for fq in range(4):
        gu_ref[:, fq * C : (fq + 1) * C] = wpack[16 + 4 * fq : 20 + 4 * fq, :]

    arrive(PY, rpy.at[pl.ds(0, Y - 1)])
    rpy[y] = jnp.zeros((NQ * 8, LY), bf16)
    total = (ppart[core, y] + rpc[y]).reshape(NQ * 8, LY)
    for s in range(Y):
        total = total + rpy[s].astype(f32)
    spq[...] = total.reshape(NQ, 8, LY)

    def send_pq(d):
        peer = lax.rem(q + d, NQ)
        push(PQ, spq.at[peer], rpq.at[q], 2 * peer + core, y)

    each(NQ, send_pq)

    arrive(TY, rty.at[pl.ds(0, Y - 1)])
    rt2[core, z] = rty[...].sum(axis=0)
    each(Z, lambda d: push(TZ2, rt2.at[core, z], rt2.at[core, z], tok_of(xx, lax.rem(z + d, Z)), y))

    for i in range(2):
        d_grid = mm(f1t[0], df[0, i]) + mm(f1t[1], df[1, i])
        gx_ref[i] = gx_ref[i] + d_grid.reshape(NQ, 2, 8, C)

    arrive(PQ, rpq.at[pl.ds(0, NQ - 1)])
    rpq[q] = spq[q]
    fin[q] = rpq[...].sum(axis=0).astype(bf16).astype(f32)
    each(NQ, lambda d: push(PQ2, fin.at[q], fin.at[q], 2 * lax.rem(q + d, NQ) + core, y))

    arrive(TZ2, rt2.at[core, pl.ds(0, Z - 1)])
    push(TC2, rt2.at[core], rt2.at[core], sib, y)

    arrive(PQ2, fin.at[pl.ds(0, NQ - 1)])
    fy[core, y] = fin[...].reshape(NQ * 8, LY).astype(bf16)
    each(Y, lambda d: push(PY2, fy.at[core, y], fy.at[core, y], t, lax.rem(y + d, Y)))
    arrive(TC2, rt2.at[other])
    g2_ref[...] = rt2[...].reshape(R, R)
    arrive(PY2, fy.at[core, pl.ds(0, Y - 1)])
    push(PC2, fy.at[core], fy.at[core], sib, y)
    arrive(PC2, fy.at[other])

    for which, phase in ((A1, 0), (A2 + core, 1), (A3, 2), (A4 + core, 3)):
        sent(which, sa.at[phase, pl.ds(0, nt - 1)])
    sent(WZ, wbuf.at[0, 0, pl.ds(0, Z - 1)])
    sent(WX, wbuf.at[0, pl.ds(0, X - 1)])
    sent(WC, wbuf.at[0])
    sent(GC, rgc)
    sent(GX, sgx.at[pl.ds(0, X - 1)])
    sent(GZ, sgz.at[pl.ds(0, Z - 1)])
    sent(TC, rtc)
    sent(TZ, stz.at[pl.ds(0, Z - 1)])
    sent(TX, rtx.at[pl.ds(0, X - 1)])
    sent(TY, rty.at[pl.ds(0, Y - 1)])
    sent(TZ2, rt2.at[0, pl.ds(0, Z - 1)])
    sent(TC2, rt2.at[0])
    sent(PC, rpc)
    sent(PY, spy.at[pl.ds(0, Y - 1)])
    sent(PQ, spq.at[pl.ds(0, NQ - 1)])
    sent(PQ2, fin.at[pl.ds(0, NQ - 1)])
    sent(PY2, fy.at[0, pl.ds(0, Y - 1)])
    sent(PC2, fy.at[0])


def deliver(Y, out_in, gx_in, fy_in, g2_in, gu_in, gd_in,
            out_ref, gx_ref, g1_ref, g2_ref, gu_ref, gd_ref, whole, sem):
    copies = [pltpu.make_async_copy(src, dst, sem.at[n]) for n, (src, dst) in enumerate(
        ((out_in, out_ref), (gx_in, gx_ref), (g2_in, g2_ref), (gu_in, gu_ref), (gd_in, gd_ref)))]
    for copy in copies:
        copy.start()
    NQ = whole.shape[0]
    LY = whole.shape[3] // Y
    for c in range(2):
        for v in range(Y):
            whole[:, c, :, v * LY : (v + 1) * LY] = fy_in[c, v].astype(f32).reshape(NQ, 8, LY)
    last = pltpu.make_async_copy(whole, g1_ref, sem.at[5])
    last.start()
    for copy in copies:
        copy.wait()
    last.wait()


def local(X, Z, Y, inputs, factor_one, twiddle, factor_two, w_up, w_down, out_cotangent):
    NQ = X * Z
    nt = 2 * NQ
    C = inputs.shape[1]
    M = 8 * nt
    H = 8 * NQ
    N = 16 * nt
    R = 2 * nt
    LY = M // Y
    W = min(C, 128)
    V = pltpu.VMEM
    whole = (2, NQ, 2, 8, C)
    scratch = [
        V(whole, f32), V((M, M), f32), V(whole, f32), V((2, M), f32), V((R, R), f32),
        V((4, 4 * C), bf16), V((16, C), bf16),
        V((4, nt, 16, C), bf16), V((4, nt, 16, C), bf16),
        V((N, N), bf16), V((N, N), bf16), V((N, N), bf16),
        V((2, M, H), bf16), V((2, M, C), bf16), V((2, NQ, 2, 8, 1), f32),
        V((2, X, Z, 32, C), bf16), V((C, 4 * C), bf16), V((NQ, 2, 16, C), bf16),
        V((C, W), f32), V((C // W, N, W), f32),
        V((N, 4 * C), f32), V((N, 4 * C), bf16), V((N, 4 * C), bf16), V((N, C), bf16), V((N, C), bf16),
        V((2, 2, H, C), bf16),
        V((2, NQ, 32, C), f32), V((NQ, 32, C), f32),
        V((X, Z, 32, C), bf16), V((X, Z, 32, C), bf16), V((Z, 32, C), bf16), V((Z, 32, C), bf16),
        V((R, R), f32), V((2, nt, R), f32), V((nt, R), f32),
        V((Z, nt // Z, R), f32), V((Z, nt // Z, R), f32), V((X, nt // Z, R), f32), V((Y, nt // Z, R), f32),
        V((2, Z, nt // Z, R), f32),
        V((2, Y, NQ, 8, LY), f32), V((Y, NQ, 8, LY), f32),
        V((Y, NQ * 8, LY), bf16), V((Y, NQ * 8, LY), bf16),
        V((NQ, 8, LY), f32), V((NQ, 8, LY), f32), V((NQ, 8, LY), f32),
        V((32, C), f32),
        pltpu.SemaphoreType.DMA((NEX,)), pltpu.SemaphoreType.DMA((NEX,)), pltpu.SemaphoreType.DMA((7,)),
    ]
    small = [((R, R), f32), ((4, 4 * C), f32), ((16, C), f32)]
    held = [(whole, f32), (whole, f32), ((2, Y, NQ * 8, LY), bf16)] + small
    final = [(whole, f32), (whole, f32), ((NQ, 2, 8, M), f32)] + small
    vm = pl.BlockSpec(memory_space=pltpu.VMEM)
    anywhere = pl.BlockSpec(memory_space=pl.ANY)
    results = pl.pallas_call(
        functools.partial(kernel, X, Z, Y),
        out_shape=[pltpu.VMEM(*s) for s in held],
        in_specs=[anywhere] * 7,
        out_specs=[vm] * 6,
        scratch_shapes=scratch,
        compiler_params=pltpu.CompilerParams(
            collective_id=0, has_side_effects=True, vmem_limit_bytes=60 * 1024 * 1024),
        name="monarch",
    )(
        inputs.reshape(whole), factor_one, twiddle, factor_two,
        w_up[0], w_down[0], out_cotangent.reshape(whole),
    )
    out, gx, g1, g2, gu, gd = pl.pallas_call(
        functools.partial(deliver, Y),
        out_shape=[jax.ShapeDtypeStruct(*s) for s in final],
        in_specs=[vm] * 6,
        out_specs=[anywhere] * 6,
        scratch_shapes=[V((NQ, 2, 8, M), f32), pltpu.SemaphoreType.DMA((6,))],
        compiler_params=pltpu.CompilerParams(vmem_limit_bytes=8 * 1024 * 1024),
        name="deliver",
    )(*[pltpu.with_memory_space_constraint(r, pltpu.VMEM) for r in results])
    return (out.reshape(2 * M, C), gx.reshape(2 * M, C), g1.reshape(M, M), g2, gu[None], gd[None])


def solution(mesh):
    nt = mesh.shape["tok"]
    Y = mesh.shape["ch"]
    X = 4 if nt == 64 else 2
    in_specs = (
        P("tok", "ch"),
        P(),
        P("tok", None),
        P(),
        P("ch", "tok", None),
        P("ch", "tok", None),
        P("tok", "ch"),
    )
    out_specs = (
        P("tok", "ch"),
        P("tok", "ch"),
        P(),
        P(),
        P("ch", "tok", None),
        P("ch", "tok", None),
    )
    return jax.shard_map(
        functools.partial(local, X, nt // 2 // X, Y), mesh=mesh, in_specs=in_specs, out_specs=out_specs, check_vma=False)
```

```python
import functools
import math

import jax
import jax.numpy as jnp
from jax import lax
from jax.experimental import pallas as pl
from jax.experimental.pallas import tpu as pltpu
from jax.sharding import PartitionSpec as P

inv_root_two = 1.0 / math.sqrt(2.0)
inv_root_tau = 1.0 / math.sqrt(2.0 * math.pi)
f32 = jnp.float32
bf16 = jnp.bfloat16

(A1, A2, A2B, A3, A4, A4B, WZ, WX, WC, GC, GX, GZ, TC, TZ, TX, TY, TZ2, TC2, PC, PY, PQ, PQ2, PY2, PC2) = range(24)
NEX = 24
LX, LF1, LOC, LTW, LF2, LWU, LWD = range(7)


def gelu_parts(value):
    cdf = 0.5 * (1.0 + lax.erf(value * inv_root_two))
    return (value * cdf, cdf + value * jnp.exp(-0.5 * value * value) * inv_root_tau)


def mm(a, b):
    return jnp.dot(a, b, preferred_element_type=f32)


def mm_nt(a, b):
    return lax.dot_general(a, b, (((1,), (1,)), ((), ())), preferred_element_type=f32)


def mm_tn(a, b):
    return lax.dot_general(a, b, (((0,), (0,)), ((), ())), preferred_element_type=f32)


def split(a):
    high = a.astype(bf16)
    return high, (a - high.astype(f32)).astype(bf16)


def kernel(X, Z, Y, x_in, f1_in, tw_in, f2_in, wu_in, wd_in, oc_in,
           out_ref, gx_ref, fy, g2_ref, gu_ref, gd_ref,
           xv, f1v, ocv, tw_ref, f2v, wu_ref, wd_ref,
           sa, ra, kh, kth, ktl, f1t, xb, twc, wbuf, wup, wdn, stage, rows4, dhid, hid, dup, nrm, cot, df,
           gbuf, rgc, sgx, rgx, sgz, rgz, tsum, tpart, rtc, stz, rtz, rtx, rty, rt2,
           ppart, rpc, spy, rpy, spq, rpq, fin, wpack, ssem, rsem, lsem):
    NQ = X * Z
    nt = 2 * NQ
    C = xv.shape[4]
    M = 8 * nt
    H = 8 * NQ
    N = 16 * nt
    R = 2 * nt
    LY = M // Y
    W = min(C, 128)
    lgq = NQ.bit_length() - 1
    t = lax.axis_index("tok")
    y = lax.axis_index("ch")
    core = lax.rem(t, 2)
    q = lax.div(t, 2)
    z = lax.rem(q, Z)
    xx = lax.div(q, Z)
    sib = t + 1 - 2 * core
    other = 1 - core
    me = core * NQ + q

    def tok_of(x_at, z_at):
        return (x_at * Z + z_at) * 2 + core

    def push(which, src, dst, tok, ch):
        pltpu.make_async_remote_copy(
            src_ref=src, dst_ref=dst, send_sem=ssem.at[which], recv_sem=rsem.at[which],
            device_id=(tok, ch), device_id_type=pl.DeviceIdType.MESH,
        ).start()

    def arrive(which, view):
        pltpu.make_async_copy(view, view, rsem.at[which]).wait()

    def sent(which, view):
        pltpu.make_async_copy(view, view, ssem.at[which]).wait()

    def each(count, body, start=1):
        def step(d, carry):
            body(d)
            return carry
        lax.fori_loop(start, count, step, 0)

    barrier = pltpu.get_barrier_semaphore()

    def greet_tok(d):
        pl.semaphore_signal(barrier, inc=1, device_id=(lax.rem(t + d, nt), y), device_id_type=pl.DeviceIdType.MESH)

    def greet_ch(d):
        pl.semaphore_signal(barrier, inc=1, device_id=(t, lax.rem(y + d, Y)), device_id_type=pl.DeviceIdType.MESH)

    each(nt, greet_tok)
    each(Y, greet_ch)
    loads = {}
    for which, src, dst in ((LF1, f1_in, f1v), (LX, x_in, xv), (LTW, tw_in, tw_ref), (LWU, wu_in, wu_ref),
                            (LWD, wd_in, wd_ref), (LF2, f2_in, f2v), (LOC, oc_in, ocv)):
        loads[which] = pltpu.make_async_copy(src, dst, lsem.at[which])
        loads[which].start()

    loads[LF1].wait()
    f1h, f1l = split(f1v[...])
    loads[LTW].wait()
    eye = lax.broadcasted_iota(jnp.int32, (M, M), 0) == lax.broadcasted_iota(jnp.int32, (M, M), 1)
    for i in range(2):
        col = jnp.sum(jnp.where(eye, tw_ref[i : i + 1, :], 0.0), axis=1, keepdims=True)
        twc[i] = col.reshape(NQ, 2, 8, 1)

    def pair(a, b):
        n = a.shape[0]
        return jnp.concatenate([a[:, None], b[:, None]], axis=1).reshape(n, 16, C)

    loads[LX].wait()
    mids = []
    for i in range(2):
        xh, xl = split(xv[i].reshape(M, C))
        xb[i] = xh
        first = mm(f1h, xh) + mm(f1h, xl) + mm(f1l, xh)
        mids.append(first.reshape(NQ, 2, 8, C) * twc[i])
    for c in range(2):
        sa[0, c * NQ : (c + 1) * NQ] = pair(mids[0][:, c], mids[1][:, c]).astype(bf16)
    ra[0, me] = sa[0, me]

    loads[LWU].wait()
    loads[LWD].wait()
    wpack[...] = jnp.concatenate(
        [wd_ref[...].astype(f32)] + [wu_ref[:, fq * C : (fq + 1) * C].astype(f32) for fq in range(4)], axis=0)
    wbuf[core, xx, z] = wpack[...].astype(bf16)

    loads[LF2].wait()
    f2h = f2v[...].astype(bf16)
    f2th, f2tl = split(f2v[...].T)
    band = min(N // 2, 128)

    def row_of(n):
        return 4 * ((n >> 4) & (NQ - 1)) + 2 * (n >> (4 + lgq)) + ((n >> 3) & 1)

    spread = row_of(lax.broadcasted_iota(jnp.int32, (N, R), 0)) == lax.broadcasted_iota(jnp.int32, (N, R), 1)
    spread = jnp.where(spread, 1.0, 0.0).astype(bf16)
    same = ((lax.broadcasted_iota(jnp.int32, (band, N), 0) & 7) == (lax.broadcasted_iota(jnp.int32, (band, N), 1) & 7))

    def picked(r0):
        rows = row_of(lax.broadcasted_iota(jnp.int32, (band, R), 0) + r0)
        return jnp.where(rows == lax.broadcasted_iota(jnp.int32, (band, R), 1), 1.0, 0.0).astype(bf16)

    def build(src, dst):
        def step(b, carry):
            r0 = pl.multiple_of(b * band, band)
            part = mm_nt(mm(picked(r0), src).astype(bf16), spread)
            dst[pl.ds(r0, band), :] = jnp.where(same, part, 0.0).astype(bf16)
            return carry
        lax.fori_loop(0, N // band, step, 0)

    build(f2h, kh)

    pl.semaphore_wait(barrier, nt - 1 + Y - 1)

    def a2a(phase, which):
        for c in range(2):
            def one(d):
                peer = lax.rem(q + d, NQ)

                @pl.when((peer != q) | (core != c))
                def _():
                    push(which, sa.at[phase, c * NQ + peer], ra.at[phase, me], 2 * peer + c, y)

            each(NQ, one, 0)

    def from_core(which, phase, c):
        @pl.when(core == c)
        def _():
            arrive(which, ra.at[phase, pl.ds(0, NQ - 1)])

        @pl.when(core != c)
        def _():
            arrive(which, ra.at[phase, pl.ds(0, NQ)])

    def from_all(which, phase):
        arrive(which, ra.at[phase, pl.ds(0, nt - 1)])

    each(Z, lambda d: push(WZ, wbuf.at[core, xx, z], wbuf.at[core, xx, z], tok_of(xx, lax.rem(z + d, Z)), y))
    a2a(0, A1)
    build(f2th, kth)

    arrive(WZ, wbuf.at[core, xx, pl.ds(0, Z - 1)])
    each(X, lambda d: push(WX, wbuf.at[core, xx], wbuf.at[core, xx], tok_of(lax.rem(xx + d, X), z), y))

    build(f2tl, ktl)
    from_all(A1, 0)
    sa[1] = mm(kh[...], ra[0].reshape(N, C)).astype(bf16).reshape(nt, 16, C)
    ra[1, me] = sa[1, me]
    a2a(1, A2 + core)

    arrive(WX, wbuf.at[core, pl.ds(0, X - 1)])
    push(WC, wbuf.at[core], wbuf.at[core], sib, y)
    for c in range(2):
        f1t[c] = f1v[...].reshape(NQ, 2, 8, M)[:, c].reshape(H, M).T.astype(bf16)
    arrive(WC, wbuf.at[other])

    for c in range(2):
        wdn[:, c] = wbuf[c, :, :, 0:16].reshape(NQ, 16, C)
    up_rows = [wbuf[c, :, :, 16:32].astype(f32).reshape(NQ, 1, 16, C) for c in range(2)]
    up_rows = jnp.concatenate(up_rows, axis=1).reshape(N, C)
    for h in range(C // W):
        rows4[h] = up_rows[:, h * W : (h + 1) * W]
    for fq in range(4):
        for h in range(C // W):
            for r in range(4):
                stage[pl.ds(r, nt, stride=4), :] = rows4[h, pl.ds(4 * fq + r, nt, stride=16), :]
            wup[:, fq * C + h * W : fq * C + (h + 1) * W] = stage[...].astype(bf16)

    nb = max(1, NQ // 2)
    tiles = NQ // nb
    TB = nb * 16

    def tokens(ref, c, q0):
        return pair(ref[0, pl.ds(q0, nb), c], ref[1, pl.ds(q0, nb), c]).reshape(TB, C)

    def put(ref, c, q0, value):
        value = value.reshape(nb, 2, 8, C)
        ref[0, pl.ds(q0, nb), c] = value[:, 0]
        ref[1, pl.ds(q0, nb), c] = value[:, 1]

    def places(c, j):
        q0 = pl.multiple_of(j * nb, nb)
        return q0, pl.ds(pl.multiple_of(c * H * 2 + j * TB, TB), TB)

    loads[LOC].wait()
    for c in range(2):
        def pre(j, carry):
            q0, rows = places(c, j)
            c16 = tokens(ocv, c, q0).astype(bf16)
            cot[rows, :] = c16
            dhid[rows, :] = mm_nt(c16, wdn[...].reshape(N, C))
            return carry

        lax.fori_loop(0, tiles, pre, 0)

    for c in range(2):
        from_core(A2 + c, 1, c)

        def mlp(j, carry):
            tile = lax.rem(lax.div(q, nb) + j, tiles)
            q0, rows = places(c, tile)
            mixed = ra[1, pl.ds(c * NQ + q0, nb)].reshape(TB, C).astype(f32)
            inp = tokens(xv, c, q0)
            gate = jax.nn.sigmoid(inp)
            branch = inp + gate * mixed
            put(out_ref, c, q0, branch)
            normed = branch.astype(bf16)
            nrm[rows, :] = normed
            up = mm(normed, wup[...])
            active, slope = gelu_parts(up)
            hid[rows, :] = active.astype(bf16)
            d_up = (dhid[rows, :] * slope).astype(bf16)
            dup[rows, :] = d_up
            d_branch = tokens(ocv, c, q0) + mm_nt(d_up, wup[...])
            sa[2, pl.ds(c * NQ + q0, nb)] = (d_branch * gate).astype(bf16).reshape(nb, 16, C)

            def one(b, inner):
                peer = q0 + lax.rem(q + b, nb)

                @pl.when((peer != q) | (core != c))
                def _():
                    push(A3, sa.at[2, c * NQ + peer], ra.at[2, me], 2 * peer + c, y)

                return inner

            lax.fori_loop(0, nb, one, 0)
            put(gx_ref, c, q0, d_branch * (1.0 + gate * (1.0 - gate) * mixed))
            return carry

        lax.fori_loop(0, tiles, mlp, 0)
    ra[2, me] = sa[2, me]

    from_all(A3, 2)
    grad = ra[2].reshape(N, C)
    sa[3] = (mm(kth[...], grad) + mm(ktl[...], grad)).astype(bf16).reshape(nt, 16, C)
    ra[3, me] = sa[3, me]
    a2a(3, A4 + core)

    gd_part = mm_tn(hid[...], cot[...]).reshape(NQ, 2, 16, C)
    for c in range(2):
        gbuf[c, :, 0:16] = gd_part[:, c]
    for fq in range(4):
        gu_part = mm_tn(nrm[...], dup[:, fq * C : (fq + 1) * C])
        for h in range(C // W):
            stage[...] = gu_part[:, h * W : (h + 1) * W]
            for r in range(4):
                rows4[h, pl.ds(4 * fq + r, nt, stride=16), :] = stage[pl.ds(r, nt, stride=4), :]
    for c in range(2):
        for h in range(C // W):
            gbuf[c, :, 16:32, h * W : (h + 1) * W] = rows4[h].reshape(NQ, 2, 16, W)[:, c]
    push(GC, gbuf.at[other], rgc, sib, y)

    tsum[...] = jnp.zeros((R, R), f32)

    def two(b, carry):
        r0 = pl.multiple_of(b * band, band)
        blocks = ra[2, pl.ds(b * (band // 16), band // 16)]
        prod = mm_nt(blocks.reshape(band, C), ra[0].reshape(N, C))
        ph, pw = split(jnp.where(same, prod, 0.0))
        ph, pw = split(mm(ph, spread) + mm(pw, spread))
        tsum[...] += mm_tn(picked(r0), ph) + mm_tn(picked(r0), pw)
        return carry

    lax.fori_loop(0, N // band, two, 0)
    tpart[...] = tsum[...].reshape(2, nt, R)
    push(TC, tpart.at[other], rtc, sib, y)

    arrive(GC, rgc)
    sgx[...] = (gbuf[core] + rgc[...]).astype(bf16).reshape(X, Z, 32, C)

    def send_gx(d):
        peer = lax.rem(xx + d, X)
        push(GX, sgx.at[peer], rgx.at[xx], tok_of(peer, z), y)

    each(X, send_gx)

    arrive(TC, rtc)
    stz[...] = (tpart[core] + rtc[...]).reshape(Z, nt // Z, R)

    def send_tz(d):
        peer = lax.rem(z + d, Z)
        push(TZ, stz.at[peer], rtz.at[z], tok_of(xx, peer), y)

    each(Z, send_tz)

    for c in range(2):
        from_core(A4 + c, 3, c)
        d_mid = ra[3, c * NQ : (c + 1) * NQ].astype(f32).reshape(NQ, 2, 8, C)
        one = None
        for i in range(2):
            d_first = (d_mid[:, i] * twc[i, :, c]).reshape(H, C).astype(bf16)
            df[c, i] = d_first
            part = mm_nt(d_first, xb[i])
            one = part if one is None else one + part
        one = one.reshape(NQ, 8, M)
        for v in range(Y):
            ppart[c, v] = one[:, :, v * LY : (v + 1) * LY]

        @pl.when(core != c)
        def _():
            push(PC, ppart.at[c], rpc, sib, y)

    for c in range(2):
        def finish(j, carry):
            q0, rows = places(c, j)
            put(out_ref, c, q0, tokens(out_ref, c, q0) + mm(hid[rows, :], wdn[...].reshape(N, C)))
            return carry

        lax.fori_loop(0, tiles, finish, 0)

    arrive(PC, rpc)
    spy[...] = (ppart[core] + rpc[...]).astype(bf16).reshape(Y, NQ * 8, LY)

    def send_py(d):
        peer = lax.rem(y + d, Y)
        push(PY, spy.at[peer], rpy.at[y], t, peer)

    each(Y, send_py)

    arrive(GX, rgx.at[pl.ds(0, X - 1)])
    rgx[xx] = jnp.zeros((Z, 32, C), bf16)
    zrows = pl.ds(xx * Z, Z)
    own_gz = gbuf[core, zrows] + rgc[zrows]
    for s in range(X):
        own_gz = own_gz + rgx[s].astype(f32)
    gbuf[core, zrows] = own_gz
    sgz[...] = own_gz.astype(bf16)

    def send_gz(d):
        peer = lax.rem(z + d, Z)
        push(GZ, sgz.at[peer], rgz.at[z], tok_of(xx, peer), y)

    each(Z, send_gz)

    arrive(TZ, rtz.at[pl.ds(0, Z - 1)])
    rtz[z] = stz[z]
    rtx[xx] = rtz[...].sum(axis=0)
    each(X, lambda d: push(TX, rtx.at[xx], rtx.at[xx], tok_of(lax.rem(xx + d, X), z), y))

    arrive(PY, rpy.at[pl.ds(0, Y - 1)])
    rpy[y] = jnp.zeros((NQ * 8, LY), bf16)
    total = (ppart[core, y] + rpc[y]).reshape(NQ * 8, LY)
    for s in range(Y):
        total = total + rpy[s].astype(f32)
    spq[...] = total.reshape(NQ, 8, LY)

    def send_pq(d):
        peer = lax.rem(q + d, NQ)
        push(PQ, spq.at[peer], rpq.at[q], 2 * peer + core, y)

    each(NQ, send_pq)

    for i in range(2):
        d_grid = mm(f1t[0], df[0, i]) + mm(f1t[1], df[1, i])
        gx_ref[i] = gx_ref[i] + d_grid.reshape(NQ, 2, 8, C)

    arrive(TX, rtx.at[pl.ds(0, X - 1)])
    rty[y] = rtx[...].sum(axis=0)
    each(Y, lambda d: push(TY, rty.at[y], rty.at[y], t, lax.rem(y + d, Y)))

    arrive(GZ, rgz.at[pl.ds(0, Z - 1)])
    rgz[z] = jnp.zeros((32, C), bf16)
    wpack[...] = gbuf[core, xx * Z + z] + rgz[...].astype(f32).sum(axis=0)
    gd_ref[...] = wpack[0:16, :]
    for fq in range(4):
        gu_ref[:, fq * C : (fq + 1) * C] = wpack[16 + 4 * fq : 20 + 4 * fq, :]

    arrive(PQ, rpq.at[pl.ds(0, NQ - 1)])
    rpq[q] = spq[q]
    fin[q] = rpq[...].sum(axis=0).astype(bf16).astype(f32)
    each(NQ, lambda d: push(PQ2, fin.at[q], fin.at[q], 2 * lax.rem(q + d, NQ) + core, y))

    arrive(TY, rty.at[pl.ds(0, Y - 1)])
    rt2[core, z] = rty[...].sum(axis=0)
    each(Z, lambda d: push(TZ2, rt2.at[core, z], rt2.at[core, z], tok_of(xx, lax.rem(z + d, Z)), y))

    arrive(PQ2, fin.at[pl.ds(0, NQ - 1)])
    fy[core, y] = fin[...].reshape(NQ * 8, LY).astype(bf16)
    each(Y, lambda d: push(PY2, fy.at[core, y], fy.at[core, y], t, lax.rem(y + d, Y)))
    arrive(TZ2, rt2.at[core, pl.ds(0, Z - 1)])
    push(TC2, rt2.at[core], rt2.at[core], sib, y)
    arrive(PY2, fy.at[core, pl.ds(0, Y - 1)])
    push(PC2, fy.at[core], fy.at[core], sib, y)
    arrive(TC2, rt2.at[other])
    g2_ref[...] = rt2[...].reshape(R, R)
    arrive(PC2, fy.at[other])

    for which, phase in ((A1, 0), (A2 + core, 1), (A3, 2), (A4 + core, 3)):
        sent(which, sa.at[phase, pl.ds(0, nt - 1)])
    sent(WZ, wbuf.at[0, 0, pl.ds(0, Z - 1)])
    sent(WX, wbuf.at[0, pl.ds(0, X - 1)])
    sent(WC, wbuf.at[0])
    sent(GC, rgc)
    sent(GX, sgx.at[pl.ds(0, X - 1)])
    sent(GZ, sgz.at[pl.ds(0, Z - 1)])
    sent(TC, rtc)
    sent(TZ, stz.at[pl.ds(0, Z - 1)])
    sent(TX, rtx.at[pl.ds(0, X - 1)])
    sent(TY, rty.at[pl.ds(0, Y - 1)])
    sent(TZ2, rt2.at[0, pl.ds(0, Z - 1)])
    sent(TC2, rt2.at[0])
    sent(PC, rpc)
    sent(PY, spy.at[pl.ds(0, Y - 1)])
    sent(PQ, spq.at[pl.ds(0, NQ - 1)])
    sent(PQ2, fin.at[pl.ds(0, NQ - 1)])
    sent(PY2, fy.at[0, pl.ds(0, Y - 1)])
    sent(PC2, fy.at[0])


def deliver(Y, out_in, gx_in, fy_in, g2_in, gu_in, gd_in,
            out_ref, gx_ref, g1_ref, g2_ref, gu_ref, gd_ref, whole, sem):
    copies = [pltpu.make_async_copy(src, dst, sem.at[n]) for n, (src, dst) in enumerate(
        ((out_in, out_ref), (gx_in, gx_ref), (g2_in, g2_ref), (gu_in, gu_ref), (gd_in, gd_ref)))]
    for copy in copies:
        copy.start()
    NQ = whole.shape[0]
    LY = whole.shape[3] // Y
    for c in range(2):
        for v in range(Y):
            whole[:, c, :, v * LY : (v + 1) * LY] = fy_in[c, v].astype(f32).reshape(NQ, 8, LY)
    last = pltpu.make_async_copy(whole, g1_ref, sem.at[5])
    last.start()
    for copy in copies:
        copy.wait()
    last.wait()


def local(X, Z, Y, inputs, factor_one, twiddle, factor_two, w_up, w_down, out_cotangent):
    NQ = X * Z
    nt = 2 * NQ
    C = inputs.shape[1]
    M = 8 * nt
    H = 8 * NQ
    N = 16 * nt
    R = 2 * nt
    LY = M // Y
    W = min(C, 128)
    V = pltpu.VMEM
    whole = (2, NQ, 2, 8, C)
    scratch = [
        V(whole, f32), V((M, M), f32), V(whole, f32), V((2, M), f32), V((R, R), f32),
        V((4, 4 * C), bf16), V((16, C), bf16),
        V((4, nt, 16, C), bf16), V((4, nt, 16, C), bf16),
        V((N, N), bf16), V((N, N), bf16), V((N, N), bf16),
        V((2, M, H), bf16), V((2, M, C), bf16), V((2, NQ, 2, 8, 1), f32),
        V((2, X, Z, 32, C), bf16), V((C, 4 * C), bf16), V((NQ, 2, 16, C), bf16),
        V((C, W), f32), V((C // W, N, W), f32),
        V((N, 4 * C), f32), V((N, 4 * C), bf16), V((N, 4 * C), bf16), V((N, C), bf16), V((N, C), bf16),
        V((2, 2, H, C), bf16),
        V((2, NQ, 32, C), f32), V((NQ, 32, C), f32),
        V((X, Z, 32, C), bf16), V((X, Z, 32, C), bf16), V((Z, 32, C), bf16), V((Z, 32, C), bf16),
        V((R, R), f32), V((2, nt, R), f32), V((nt, R), f32),
        V((Z, nt // Z, R), f32), V((Z, nt // Z, R), f32), V((X, nt // Z, R), f32), V((Y, nt // Z, R), f32),
        V((2, Z, nt // Z, R), f32),
        V((2, Y, NQ, 8, LY), f32), V((Y, NQ, 8, LY), f32),
        V((Y, NQ * 8, LY), bf16), V((Y, NQ * 8, LY), bf16),
        V((NQ, 8, LY), f32), V((NQ, 8, LY), f32), V((NQ, 8, LY), f32),
        V((32, C), f32),
        pltpu.SemaphoreType.DMA((NEX,)), pltpu.SemaphoreType.DMA((NEX,)), pltpu.SemaphoreType.DMA((7,)),
    ]
    small = [((R, R), f32), ((4, 4 * C), f32), ((16, C), f32)]
    held = [(whole, f32), (whole, f32), ((2, Y, NQ * 8, LY), bf16)] + small
    final = [(whole, f32), (whole, f32), ((NQ, 2, 8, M), f32)] + small
    vm = pl.BlockSpec(memory_space=pltpu.VMEM)
    anywhere = pl.BlockSpec(memory_space=pl.ANY)
    results = pl.pallas_call(
        functools.partial(kernel, X, Z, Y),
        out_shape=[pltpu.VMEM(*s) for s in held],
        in_specs=[anywhere] * 7,
        out_specs=[vm] * 6,
        scratch_shapes=scratch,
        compiler_params=pltpu.CompilerParams(
            collective_id=0, has_side_effects=True, vmem_limit_bytes=60 * 1024 * 1024),
        name="monarch",
    )(
        inputs.reshape(whole), factor_one, twiddle, factor_two,
        w_up[0], w_down[0], out_cotangent.reshape(whole),
    )
    out, gx, g1, g2, gu, gd = pl.pallas_call(
        functools.partial(deliver, Y),
        out_shape=[jax.ShapeDtypeStruct(*s) for s in final],
        in_specs=[vm] * 6,
        out_specs=[anywhere] * 6,
        scratch_shapes=[V((NQ, 2, 8, M), f32), pltpu.SemaphoreType.DMA((6,))],
        compiler_params=pltpu.CompilerParams(vmem_limit_bytes=8 * 1024 * 1024),
        name="deliver",
    )(*[pltpu.with_memory_space_constraint(r, pltpu.VMEM) for r in results])
    return (out.reshape(2 * M, C), gx.reshape(2 * M, C), g1.reshape(M, M), g2, gu[None], gd[None])


def solution(mesh):
    nt = mesh.shape["tok"]
    Y = mesh.shape["ch"]
    X = 4 if nt == 64 else 2
    in_specs = (
        P("tok", "ch"),
        P(),
        P("tok", None),
        P(),
        P("ch", "tok", None),
        P("ch", "tok", None),
        P("tok", "ch"),
    )
    out_specs = (
        P("tok", "ch"),
        P("tok", "ch"),
        P(),
        P(),
        P("ch", "tok", None),
        P("ch", "tok", None),
    )
    return jax.shard_map(
        functools.partial(local, X, nt // 2 // X, Y), mesh=mesh, in_specs=in_specs, out_specs=out_specs, check_vma=False)
```

```python
import functools
import math

import jax
import jax.numpy as jnp
from jax import lax
from jax.experimental import pallas as pl
from jax.experimental.pallas import tpu as pltpu
from jax.sharding import PartitionSpec as P

inv_root_two = 1.0 / math.sqrt(2.0)
inv_root_tau = 1.0 / math.sqrt(2.0 * math.pi)
f32 = jnp.float32
bf16 = jnp.bfloat16

(A1, A2, A2B, A3, A4, A4B, WZ, WX, WC, GC, GX, GZ, TC, TZ, TX, TY, TZ2, TC2, PC, PY, PQ, PQ2, PY2, PC2) = range(24)
NEX = 24
LX, LF1, LOC, LTW, LF2, LWU, LWD = range(7)


def gelu_parts(value):
    cdf = 0.5 * (1.0 + lax.erf(value * inv_root_two))
    return (value * cdf, cdf + value * jnp.exp(-0.5 * value * value) * inv_root_tau)


def mm(a, b):
    return jnp.dot(a, b, preferred_element_type=f32)


def mm_nt(a, b):
    return lax.dot_general(a, b, (((1,), (1,)), ((), ())), preferred_element_type=f32)


def mm_tn(a, b):
    return lax.dot_general(a, b, (((0,), (0,)), ((), ())), preferred_element_type=f32)


def split(a):
    high = a.astype(bf16)
    return high, (a - high.astype(f32)).astype(bf16)


def kernel(X, Z, Y, x_in, f1_in, tw_in, f2_in, wu_in, wd_in, oc_in,
           out_ref, gx_ref, fy, g2_ref, gu_ref, gd_ref,
           xv, f1v, ocv, tw_ref, f2v, wu_ref, wd_ref,
           sa, ra, kh, kth, ktl, f1t, xb, xs, twc, wbuf, wup, wdn, stage, rows4, dhid, hid, dup, nrm, cot, df,
           gbuf, rgc, sgx, rgx, sgz, rgz, tsum, tpart, rtc, stz, rtz, rtx, rty, rt2,
           pown, spc, rpc, spy, rpy, spq, rpq, wpack, ssem, rsem, lsem):
    NQ = X * Z
    nt = 2 * NQ
    C = xv.shape[4]
    M = 8 * nt
    H = 8 * NQ
    N = 16 * nt
    R = 2 * nt
    LY = M // Y
    W = min(C, 128)
    lgq = NQ.bit_length() - 1
    t = lax.axis_index("tok")
    y = lax.axis_index("ch")
    core = lax.rem(t, 2)
    q = lax.div(t, 2)
    z = lax.rem(q, Z)
    xx = lax.div(q, Z)
    sib = t + 1 - 2 * core
    other = 1 - core
    me = core * NQ + q

    def tok_of(x_at, z_at):
        return (x_at * Z + z_at) * 2 + core

    def push(which, src, dst, tok, ch):
        pltpu.make_async_remote_copy(
            src_ref=src, dst_ref=dst, send_sem=ssem.at[which], recv_sem=rsem.at[which],
            device_id=(tok, ch), device_id_type=pl.DeviceIdType.MESH,
        ).start()

    def arrive(which, view):
        pltpu.make_async_copy(view, view, rsem.at[which]).wait()

    def sent(which, view):
        pltpu.make_async_copy(view, view, ssem.at[which]).wait()

    def each(count, body, start=1):
        def step(d, carry):
            body(d)
            return carry
        lax.fori_loop(start, count, step, 0)

    barrier = pltpu.get_barrier_semaphore()

    def greet_tok(d):
        pl.semaphore_signal(barrier, inc=1, device_id=(lax.rem(t + d, nt), y), device_id_type=pl.DeviceIdType.MESH)

    def greet_ch(d):
        pl.semaphore_signal(barrier, inc=1, device_id=(t, lax.rem(y + d, Y)), device_id_type=pl.DeviceIdType.MESH)

    each(nt, greet_tok)
    each(Y, greet_ch)
    loads = {}
    for which, src, dst in ((LF1, f1_in, f1v), (LX, x_in, xv), (LTW, tw_in, tw_ref), (LWU, wu_in, wu_ref),
                            (LWD, wd_in, wd_ref), (LF2, f2_in, f2v), (LOC, oc_in, ocv)):
        loads[which] = pltpu.make_async_copy(src, dst, lsem.at[which])
        loads[which].start()

    loads[LF1].wait()
    f1h, f1l = split(f1v[...])
    loads[LTW].wait()
    eye = lax.broadcasted_iota(jnp.int32, (M, M), 0) == lax.broadcasted_iota(jnp.int32, (M, M), 1)
    for i in range(2):
        col = jnp.sum(jnp.where(eye, tw_ref[i : i + 1, :], 0.0), axis=1, keepdims=True)
        twc[i] = col.reshape(NQ, 2, 8, 1)

    def pair(a, b):
        n = a.shape[0]
        return jnp.concatenate([a[:, None], b[:, None]], axis=1).reshape(n, 16, C)

    loads[LX].wait()
    mids = []
    for i in range(2):
        xh, xl = split(xv[i].reshape(M, C))
        xb[i] = xh
        xs[i] = xl
        first = mm(f1h, xh) + mm(f1h, xl) + mm(f1l, xh)
        mids.append(first.reshape(NQ, 2, 8, C) * twc[i])
    for c in range(2):
        sa[0, c * NQ : (c + 1) * NQ] = pair(mids[0][:, c], mids[1][:, c]).astype(bf16)
    ra[0, me] = sa[0, me]

    loads[LWU].wait()
    loads[LWD].wait()
    wpack[...] = jnp.concatenate(
        [wd_ref[...].astype(f32)] + [wu_ref[:, fq * C : (fq + 1) * C].astype(f32) for fq in range(4)], axis=0)
    wbuf[core, xx, z] = wpack[...].astype(bf16)

    pl.semaphore_wait(barrier, nt - 1 + Y - 1)

    def a2a(phase, which):
        for c in range(2):
            def one(d):
                peer = lax.rem(q + d, NQ)

                @pl.when((peer != q) | (core != c))
                def _():
                    push(which, sa.at[phase, c * NQ + peer], ra.at[phase, me], 2 * peer + c, y)

            each(NQ, one, 0)

    def from_core(which, phase, c):
        @pl.when(core == c)
        def _():
            arrive(which, ra.at[phase, pl.ds(0, NQ - 1)])

        @pl.when(core != c)
        def _():
            arrive(which, ra.at[phase, pl.ds(0, NQ)])

    def from_all(which, phase):
        arrive(which, ra.at[phase, pl.ds(0, nt - 1)])

    each(Z, lambda d: push(WZ, wbuf.at[core, xx, z], wbuf.at[core, xx, z], tok_of(xx, lax.rem(z + d, Z)), y))
    a2a(0, A1)

    loads[LF2].wait()
    f2h = f2v[...].astype(bf16)
    f2th, f2tl = split(f2v[...].T)
    band = min(N // 2, 128)

    def row_of(n):
        return 4 * ((n >> 4) & (NQ - 1)) + 2 * (n >> (4 + lgq)) + ((n >> 3) & 1)

    spread = row_of(lax.broadcasted_iota(jnp.int32, (N, R), 0)) == lax.broadcasted_iota(jnp.int32, (N, R), 1)
    spread = jnp.where(spread, 1.0, 0.0).astype(bf16)
    same = ((lax.broadcasted_iota(jnp.int32, (band, N), 0) & 7) == (lax.broadcasted_iota(jnp.int32, (band, N), 1) & 7))

    def picked(r0):
        rows = row_of(lax.broadcasted_iota(jnp.int32, (band, R), 0) + r0)
        return jnp.where(rows == lax.broadcasted_iota(jnp.int32, (band, R), 1), 1.0, 0.0).astype(bf16)

    def build(src, dst):
        def step(b, carry):
            r0 = pl.multiple_of(b * band, band)
            part = mm_nt(mm(picked(r0), src).astype(bf16), spread)
            dst[pl.ds(r0, band), :] = jnp.where(same, part, 0.0).astype(bf16)
            return carry
        lax.fori_loop(0, N // band, step, 0)

    build(f2h, kh)
    build(f2th, kth)

    arrive(WZ, wbuf.at[core, xx, pl.ds(0, Z - 1)])
    each(X, lambda d: push(WX, wbuf.at[core, xx], wbuf.at[core, xx], tok_of(lax.rem(xx + d, X), z), y))

    from_all(A1, 0)
    sa[1] = mm(kh[...], ra[0].reshape(N, C)).astype(bf16).reshape(nt, 16, C)
    ra[1, me] = sa[1, me]
    a2a(1, A2 + core)

    arrive(WX, wbuf.at[core, pl.ds(0, X - 1)])
    push(WC, wbuf.at[core], wbuf.at[core], sib, y)
    build(f2tl, ktl)
    for c in range(2):
        f1t[c] = f1v[...].reshape(NQ, 2, 8, M)[:, c].reshape(H, M).T.astype(bf16)
    arrive(WC, wbuf.at[other])

    for c in range(2):
        wdn[:, c] = wbuf[c, :, :, 0:16].reshape(NQ, 16, C)
    up_rows = [wbuf[c, :, :, 16:32].astype(f32).reshape(NQ, 1, 16, C) for c in range(2)]
    up_rows = jnp.concatenate(up_rows, axis=1).reshape(N, C)
    for h in range(C // W):
        rows4[h] = up_rows[:, h * W : (h + 1) * W]
    for fq in range(4):
        for h in range(C // W):
            for r in range(4):
                stage[pl.ds(r, nt, stride=4), :] = rows4[h, pl.ds(4 * fq + r, nt, stride=16), :]
            wup[:, fq * C + h * W : fq * C + (h + 1) * W] = stage[...].astype(bf16)

    nb = max(1, NQ // 2)
    tiles = NQ // nb
    TB = nb * 16

    def tokens(ref, c, q0):
        return pair(ref[0, pl.ds(q0, nb), c], ref[1, pl.ds(q0, nb), c]).reshape(TB, C)

    def put(ref, c, q0, value):
        value = value.reshape(nb, 2, 8, C)
        ref[0, pl.ds(q0, nb), c] = value[:, 0]
        ref[1, pl.ds(q0, nb), c] = value[:, 1]

    def places(c, j):
        q0 = pl.multiple_of(j * nb, nb)
        return q0, pl.ds(pl.multiple_of(c * H * 2 + j * TB, TB), TB)

    loads[LOC].wait()
    for c in range(2):
        def pre(j, carry):
            q0, rows = places(c, j)
            c16 = tokens(ocv, c, q0).astype(bf16)
            cot[rows, :] = c16
            dhid[rows, :] = mm_nt(c16, wdn[...].reshape(N, C))
            return carry

        lax.fori_loop(0, tiles, pre, 0)

    for c in range(2):
        from_core(A2 + c, 1, c)

        def mlp(j, carry):
            tile = lax.rem(lax.div(q, nb) + j, tiles)
            q0, rows = places(c, tile)
            mixed = ra[1, pl.ds(c * NQ + q0, nb)].reshape(TB, C).astype(f32)
            inp = tokens(xv, c, q0)
            gate = jax.nn.sigmoid(inp)
            branch = inp + gate * mixed
            put(out_ref, c, q0, branch)
            normed = branch.astype(bf16)
            nrm[rows, :] = normed
            up = mm(normed, wup[...])
            active, slope = gelu_parts(up)
            hid[rows, :] = active.astype(bf16)
            d_up = (dhid[rows, :] * slope).astype(bf16)
            dup[rows, :] = d_up
            d_branch = tokens(ocv, c, q0) + mm_nt(d_up, wup[...])
            sa[2, pl.ds(c * NQ + q0, nb)] = (d_branch * gate).astype(bf16).reshape(nb, 16, C)

            def one(b, inner):
                peer = q0 + lax.rem(q + b, nb)

                @pl.when((peer != q) | (core != c))
                def _():
                    push(A3, sa.at[2, c * NQ + peer], ra.at[2, me], 2 * peer + c, y)

                return inner

            lax.fori_loop(0, nb, one, 0)
            put(gx_ref, c, q0, d_branch * (1.0 + gate * (1.0 - gate) * mixed))
            return carry

        lax.fori_loop(0, tiles, mlp, 0)
    ra[2, me] = sa[2, me]

    from_all(A3, 2)
    grad = ra[2].reshape(N, C)
    sa[3] = (mm(kth[...], grad) + mm(ktl[...], grad)).astype(bf16).reshape(nt, 16, C)
    ra[3, me] = sa[3, me]
    a2a(3, A4 + core)

    gd_part = mm_tn(hid[...], cot[...]).reshape(NQ, 2, 16, C)
    for c in range(2):
        gbuf[c, :, 0:16] = gd_part[:, c]
    for fq in range(4):
        gu_part = mm_tn(nrm[...], dup[:, fq * C : (fq + 1) * C])
        for h in range(C // W):
            stage[...] = gu_part[:, h * W : (h + 1) * W]
            for r in range(4):
                rows4[h, pl.ds(4 * fq + r, nt, stride=16), :] = stage[pl.ds(r, nt, stride=4), :]
    for c in range(2):
        for h in range(C // W):
            gbuf[c, :, 16:32, h * W : (h + 1) * W] = rows4[h].reshape(NQ, 2, 16, W)[:, c]
    push(GC, gbuf.at[other], rgc, sib, y)

    tsum[...] = jnp.zeros((R, R), f32)

    def two(b, carry):
        r0 = pl.multiple_of(b * band, band)
        blocks = ra[2, pl.ds(b * (band // 16), band // 16)]
        prod = mm_nt(blocks.reshape(band, C), ra[0].reshape(N, C))
        ph, pw = split(jnp.where(same, prod, 0.0))
        ph, pw = split(mm(ph, spread) + mm(pw, spread))
        tsum[...] += mm_tn(picked(r0), ph) + mm_tn(picked(r0), pw)
        return carry

    lax.fori_loop(0, N // band, two, 0)
    tpart[...] = tsum[...].reshape(2, nt, R)
    push(TC, tpart.at[other], rtc, sib, y)

    for c in range(2):
        def finish(j, carry):
            q0, rows = places(c, j)
            put(out_ref, c, q0, tokens(out_ref, c, q0) + mm(hid[rows, :], wdn[...].reshape(N, C)))
            return carry

        lax.fori_loop(0, tiles, finish, 0)

    def send_py(d):
        peer = lax.rem(y + d, Y)
        push(PY, spy.at[peer], rpy.at[y], t, peer)

    def over_cores():
        arrive(PC, rpc)
        pown[...] = pown[...] + rpc[...].astype(f32)
        spy[...] = pown[...].astype(bf16)
        each(Y, send_py)

    for c in range(2):
        from_core(A4 + c, 3, c)
        d_mid = ra[3, c * NQ : (c + 1) * NQ].astype(f32).reshape(NQ, 2, 8, C)
        one = None
        for i in range(2):
            d_first = (d_mid[:, i] * twc[i, :, c]).reshape(H, C).astype(bf16)
            df[c, i] = d_first
            part = mm_nt(d_first, xb[i]) + mm_nt(d_first, xs[i])
            one = part if one is None else one + part
        one = one.reshape(NQ, 8, M)

        @pl.when(core != c)
        def _():
            for v in range(Y):
                spc[v] = one[:, :, v * LY : (v + 1) * LY].astype(bf16)
            push(PC, spc, rpc, sib, y)

        @pl.when(core == c)
        def _():
            for v in range(Y):
                pown[v] = one[:, :, v * LY : (v + 1) * LY]

        if c == 0:
            @pl.when(core == 0)
            def _():
                over_cores()

    arrive(GC, rgc)
    sgx[...] = (gbuf[core] + rgc[...]).astype(bf16).reshape(X, Z, 32, C)

    def send_gx(d):
        peer = lax.rem(xx + d, X)
        push(GX, sgx.at[peer], rgx.at[xx], tok_of(peer, z), y)

    each(X, send_gx)

    arrive(TC, rtc)
    stz[...] = (tpart[core] + rtc[...]).reshape(Z, nt // Z, R)

    def send_tz(d):
        peer = lax.rem(z + d, Z)
        push(TZ, stz.at[peer], rtz.at[z], tok_of(xx, peer), y)

    each(Z, send_tz)

    @pl.when(core == 1)
    def _():
        over_cores()

    arrive(TZ, rtz.at[pl.ds(0, Z - 1)])
    rtz[z] = stz[z]
    rtx[xx] = rtz[...].sum(axis=0)
    each(X, lambda d: push(TX, rtx.at[xx], rtx.at[xx], tok_of(lax.rem(xx + d, X), z), y))

    arrive(PY, rpy.at[pl.ds(0, Y - 1)])
    rpy[y] = jnp.zeros((NQ, 8, LY), bf16)
    total = pown[y]
    for s in range(Y):
        total = total + rpy[s].astype(f32)
    spq[...] = total.astype(bf16)

    def send_pq(d):
        peer = lax.rem(q + d, NQ)
        push(PQ, spq.at[peer], rpq.at[q], 2 * peer + core, y)

    each(NQ, send_pq)

    for i in range(2):
        d_grid = mm(f1t[0], df[0, i]) + mm(f1t[1], df[1, i])
        gx_ref[i] = gx_ref[i] + d_grid.reshape(NQ, 2, 8, C)

    arrive(GX, rgx.at[pl.ds(0, X - 1)])
    rgx[xx] = jnp.zeros((Z, 32, C), bf16)
    zrows = pl.ds(xx * Z, Z)
    own_gz = gbuf[core, zrows] + rgc[zrows]
    for s in range(X):
        own_gz = own_gz + rgx[s].astype(f32)
    gbuf[core, zrows] = own_gz
    sgz[...] = own_gz.astype(bf16)

    def send_gz(d):
        peer = lax.rem(z + d, Z)
        push(GZ, sgz.at[peer], rgz.at[z], tok_of(xx, peer), y)

    each(Z, send_gz)

    arrive(TX, rtx.at[pl.ds(0, X - 1)])
    rty[y] = rtx[...].sum(axis=0)
    each(Y, lambda d: push(TY, rty.at[y], rty.at[y], t, lax.rem(y + d, Y)))

    arrive(PQ, rpq.at[pl.ds(0, NQ - 1)])
    rpq[q] = spq[q]
    fy[core, y, q] = rpq[...].astype(f32).sum(axis=0).astype(bf16)
    each(NQ, lambda d: push(PQ2, fy.at[core, y, q], fy.at[core, y, q], 2 * lax.rem(q + d, NQ) + core, y))

    arrive(TY, rty.at[pl.ds(0, Y - 1)])
    rt2[core, z] = rty[...].sum(axis=0)
    each(Z, lambda d: push(TZ2, rt2.at[core, z], rt2.at[core, z], tok_of(xx, lax.rem(z + d, Z)), y))

    arrive(GZ, rgz.at[pl.ds(0, Z - 1)])
    rgz[z] = jnp.zeros((32, C), bf16)
    wpack[...] = gbuf[core, xx * Z + z] + rgz[...].astype(f32).sum(axis=0)
    gd_ref[...] = wpack[0:16, :]
    for fq in range(4):
        gu_ref[:, fq * C : (fq + 1) * C] = wpack[16 + 4 * fq : 20 + 4 * fq, :]

    arrive(PQ2, fy.at[core, y, pl.ds(0, NQ - 1)])
    each(Y, lambda d: push(PY2, fy.at[core, y], fy.at[core, y], t, lax.rem(y + d, Y)))
    arrive(TZ2, rt2.at[core, pl.ds(0, Z - 1)])
    push(TC2, rt2.at[core], rt2.at[core], sib, y)
    arrive(PY2, fy.at[core, pl.ds(0, Y - 1)])
    push(PC2, fy.at[core], fy.at[core], sib, y)
    arrive(TC2, rt2.at[other])
    g2_ref[...] = rt2[...].reshape(R, R)
    arrive(PC2, fy.at[other])

    for which, phase in ((A1, 0), (A2 + core, 1), (A3, 2), (A4 + core, 3)):
        sent(which, sa.at[phase, pl.ds(0, nt - 1)])
    sent(WZ, wbuf.at[0, 0, pl.ds(0, Z - 1)])
    sent(WX, wbuf.at[0, pl.ds(0, X - 1)])
    sent(WC, wbuf.at[0])
    sent(GC, rgc)
    sent(GX, sgx.at[pl.ds(0, X - 1)])
    sent(GZ, sgz.at[pl.ds(0, Z - 1)])
    sent(TC, rtc)
    sent(TZ, stz.at[pl.ds(0, Z - 1)])
    sent(TX, rtx.at[pl.ds(0, X - 1)])
    sent(TY, rty.at[pl.ds(0, Y - 1)])
    sent(TZ2, rt2.at[0, pl.ds(0, Z - 1)])
    sent(TC2, rt2.at[0])
    sent(PC, rpc)
    sent(PY, spy.at[pl.ds(0, Y - 1)])
    sent(PQ, spq.at[pl.ds(0, NQ - 1)])
    sent(PQ2, fy.at[0, 0, pl.ds(0, NQ - 1)])
    sent(PY2, fy.at[0, pl.ds(0, Y - 1)])
    sent(PC2, fy.at[0])


def deliver(Y, out_in, gx_in, fy_in, g2_in, gu_in, gd_in,
            out_ref, gx_ref, g1_ref, g2_ref, gu_ref, gd_ref, whole, sem):
    copies = [pltpu.make_async_copy(src, dst, sem.at[n]) for n, (src, dst) in enumerate(
        ((out_in, out_ref), (gx_in, gx_ref), (g2_in, g2_ref), (gu_in, gu_ref), (gd_in, gd_ref)))]
    for copy in copies:
        copy.start()
    NQ = whole.shape[0]
    LY = whole.shape[3] // Y
    for c in range(2):
        for v in range(Y):
            whole[:, c, :, v * LY : (v + 1) * LY] = fy_in[c, v].astype(f32)
    last = pltpu.make_async_copy(whole, g1_ref, sem.at[5])
    last.start()
    for copy in copies:
        copy.wait()
    last.wait()


def local(X, Z, Y, inputs, factor_one, twiddle, factor_two, w_up, w_down, out_cotangent):
    NQ = X * Z
    nt = 2 * NQ
    C = inputs.shape[1]
    M = 8 * nt
    H = 8 * NQ
    N = 16 * nt
    R = 2 * nt
    LY = M // Y
    W = min(C, 128)
    V = pltpu.VMEM
    whole = (2, NQ, 2, 8, C)
    scratch = [
        V(whole, f32), V((M, M), f32), V(whole, f32), V((2, M), f32), V((R, R), f32),
        V((4, 4 * C), bf16), V((16, C), bf16),
        V((4, nt, 16, C), bf16), V((4, nt, 16, C), bf16),
        V((N, N), bf16), V((N, N), bf16), V((N, N), bf16),
        V((2, M, H), bf16), V((2, M, C), bf16), V((2, M, C), bf16), V((2, NQ, 2, 8, 1), f32),
        V((2, X, Z, 32, C), bf16), V((C, 4 * C), bf16), V((NQ, 2, 16, C), bf16),
        V((C, W), f32), V((C // W, N, W), f32),
        V((N, 4 * C), f32), V((N, 4 * C), bf16), V((N, 4 * C), bf16), V((N, C), bf16), V((N, C), bf16),
        V((2, 2, H, C), bf16),
        V((2, NQ, 32, C), f32), V((NQ, 32, C), f32),
        V((X, Z, 32, C), bf16), V((X, Z, 32, C), bf16), V((Z, 32, C), bf16), V((Z, 32, C), bf16),
        V((R, R), f32), V((2, nt, R), f32), V((nt, R), f32),
        V((Z, nt // Z, R), f32), V((Z, nt // Z, R), f32), V((X, nt // Z, R), f32), V((Y, nt // Z, R), f32),
        V((2, Z, nt // Z, R), f32),
        V((Y, NQ, 8, LY), f32), V((Y, NQ, 8, LY), bf16), V((Y, NQ, 8, LY), bf16),
        V((Y, NQ, 8, LY), bf16), V((Y, NQ, 8, LY), bf16),
        V((NQ, 8, LY), bf16), V((NQ, 8, LY), bf16),
        V((32, C), f32),
        pltpu.SemaphoreType.DMA((NEX,)), pltpu.SemaphoreType.DMA((NEX,)), pltpu.SemaphoreType.DMA((7,)),
    ]
    small = [((R, R), f32), ((4, 4 * C), f32), ((16, C), f32)]
    held = [(whole, f32), (whole, f32), ((2, Y, NQ, 8, LY), bf16)] + small
    final = [(whole, f32), (whole, f32), ((NQ, 2, 8, M), f32)] + small
    vm = pl.BlockSpec(memory_space=pltpu.VMEM)
    anywhere = pl.BlockSpec(memory_space=pl.ANY)
    results = pl.pallas_call(
        functools.partial(kernel, X, Z, Y),
        out_shape=[pltpu.VMEM(*s) for s in held],
        in_specs=[anywhere] * 7,
        out_specs=[vm] * 6,
        scratch_shapes=scratch,
        compiler_params=pltpu.CompilerParams(
            collective_id=0, has_side_effects=True, vmem_limit_bytes=60 * 1024 * 1024),
        name="monarch",
    )(
        inputs.reshape(whole), factor_one, twiddle, factor_two,
        w_up[0], w_down[0], out_cotangent.reshape(whole),
    )
    out, gx, g1, g2, gu, gd = pl.pallas_call(
        functools.partial(deliver, Y),
        out_shape=[jax.ShapeDtypeStruct(*s) for s in final],
        in_specs=[vm] * 6,
        out_specs=[anywhere] * 6,
        scratch_shapes=[V((NQ, 2, 8, M), f32), pltpu.SemaphoreType.DMA((6,))],
        compiler_params=pltpu.CompilerParams(vmem_limit_bytes=8 * 1024 * 1024),
        name="deliver",
    )(*[pltpu.with_memory_space_constraint(r, pltpu.VMEM) for r in results])
    return (out.reshape(2 * M, C), gx.reshape(2 * M, C), g1.reshape(M, M), g2, gu[None], gd[None])


def solution(mesh):
    nt = mesh.shape["tok"]
    Y = mesh.shape["ch"]
    X = 4 if nt == 64 else 2
    in_specs = (
        P("tok", "ch"),
        P(),
        P("tok", None),
        P(),
        P("ch", "tok", None),
        P("ch", "tok", None),
        P("tok", "ch"),
    )
    out_specs = (
        P("tok", "ch"),
        P("tok", "ch"),
        P(),
        P(),
        P("ch", "tok", None),
        P("ch", "tok", None),
    )
    return jax.shard_map(
        functools.partial(local, X, nt // 2 // X, Y), mesh=mesh, in_specs=in_specs, out_specs=out_specs, check_vma=False)
```

```python
import functools
import math

import jax
import jax.numpy as jnp
from jax import lax
from jax.experimental import pallas as pl
from jax.experimental.pallas import tpu as pltpu
from jax.sharding import PartitionSpec as P

inv_root_two = 1.0 / math.sqrt(2.0)
inv_root_tau = 1.0 / math.sqrt(2.0 * math.pi)
f32 = jnp.float32
bf16 = jnp.bfloat16

(A1, A2, A2B, A3, A4, A4B, WZ, WX, WC, GC, GX, GZ, TC, TZ, TX, TY, TZ2, TC2, PC, PY, PQ, PQ2, PY2, PC2) = range(24)
NEX = 24
LX, LF1, LOC, LTW, LF2, LWU, LWD = range(7)


def gelu_parts(value):
    cdf = 0.5 * (1.0 + lax.erf(value * inv_root_two))
    return (value * cdf, cdf + value * jnp.exp(-0.5 * value * value) * inv_root_tau)


def mm(a, b):
    return jnp.dot(a, b, preferred_element_type=f32)


def mm_nt(a, b):
    return lax.dot_general(a, b, (((1,), (1,)), ((), ())), preferred_element_type=f32)


def mm_tn(a, b):
    return lax.dot_general(a, b, (((0,), (0,)), ((), ())), preferred_element_type=f32)


def split(a):
    high = a.astype(bf16)
    return high, (a - high.astype(f32)).astype(bf16)


def kernel(X, Z, Y, x_in, f1_in, tw_in, f2_in, wu_in, wd_in, oc_in,
           out_ref, gx_ref, fy, g2_ref, gu_ref, gd_ref,
           xv, f1v, ocv, tw_ref, f2v, wu_ref, wd_ref,
           sa, ra, kh, kth, ktl, f1t, xb, xs, twc, wbuf, wup, wdn, stage, rows4, dhid, hid, dup, nrm, cot, df,
           gbuf, sgc, rgc, sgx, rgx, sgz, rgz, mid32, tpart, rtc, stz, rtz, rtx, rty, rt2,
           pown, spc, rpc, spy, rpy, spq, rpq, wpack, ssem, rsem, lsem):
    NQ = X * Z
    nt = 2 * NQ
    C = xv.shape[4]
    M = 8 * nt
    H = 8 * NQ
    N = 16 * nt
    R = 2 * nt
    LY = M // Y
    W = min(C, 128)
    lgq = NQ.bit_length() - 1
    t = lax.axis_index("tok")
    y = lax.axis_index("ch")
    core = lax.rem(t, 2)
    q = lax.div(t, 2)
    z = lax.rem(q, Z)
    xx = lax.div(q, Z)
    sib = t + 1 - 2 * core
    other = 1 - core
    me = core * NQ + q

    def tok_of(x_at, z_at):
        return (x_at * Z + z_at) * 2 + core

    def push(which, src, dst, tok, ch):
        pltpu.make_async_remote_copy(
            src_ref=src, dst_ref=dst, send_sem=ssem.at[which], recv_sem=rsem.at[which],
            device_id=(tok, ch), device_id_type=pl.DeviceIdType.MESH,
        ).start()

    def arrive(which, view):
        pltpu.make_async_copy(view, view, rsem.at[which]).wait()

    def sent(which, view):
        pltpu.make_async_copy(view, view, ssem.at[which]).wait()

    def each(count, body, start=1):
        def step(d, carry):
            body(d)
            return carry
        lax.fori_loop(start, count, step, 0)

    barrier = pltpu.get_barrier_semaphore()

    def greet_tok(d):
        pl.semaphore_signal(barrier, inc=1, device_id=(lax.rem(t + d, nt), y), device_id_type=pl.DeviceIdType.MESH)

    def greet_ch(d):
        pl.semaphore_signal(barrier, inc=1, device_id=(t, lax.rem(y + d, Y)), device_id_type=pl.DeviceIdType.MESH)

    each(nt, greet_tok)
    each(Y, greet_ch)
    loads = {}
    for which, src, dst in ((LF1, f1_in, f1v), (LX, x_in, xv), (LTW, tw_in, tw_ref), (LWU, wu_in, wu_ref),
                            (LWD, wd_in, wd_ref), (LF2, f2_in, f2v), (LOC, oc_in, ocv)):
        loads[which] = pltpu.make_async_copy(src, dst, lsem.at[which])
        loads[which].start()

    loads[LF1].wait()
    f1h, f1l = split(f1v[...])
    loads[LTW].wait()
    eye = lax.broadcasted_iota(jnp.int32, (M, M), 0) == lax.broadcasted_iota(jnp.int32, (M, M), 1)
    for i in range(2):
        col = jnp.sum(jnp.where(eye, tw_ref[i : i + 1, :], 0.0), axis=1, keepdims=True)
        twc[i] = col.reshape(NQ, 2, 8, 1)

    def pair(a, b):
        n = a.shape[0]
        return jnp.concatenate([a[:, None], b[:, None]], axis=1).reshape(n, 16, C)

    loads[LX].wait()
    mids = []
    for i in range(2):
        xh, xl = split(xv[i].reshape(M, C))
        xb[i] = xh
        xs[i] = xl
        first = mm(f1h, xh) + mm(f1h, xl) + mm(f1l, xh)
        mids.append(first.reshape(NQ, 2, 8, C) * twc[i])
    for c in range(2):
        sa[0, c * NQ : (c + 1) * NQ] = pair(mids[0][:, c], mids[1][:, c]).astype(bf16)
    ra[0, me] = sa[0, me]

    loads[LWU].wait()
    loads[LWD].wait()
    wpack[...] = jnp.concatenate(
        [wd_ref[...].astype(f32)] + [wu_ref[:, fq * C : (fq + 1) * C].astype(f32) for fq in range(4)], axis=0)
    wbuf[core, xx, z] = wpack[...].astype(bf16)

    pl.semaphore_wait(barrier, nt - 1 + Y - 1)

    def a2a(phase, which):
        for c in range(2):
            def one(d):
                peer = lax.rem(q + d, NQ)

                @pl.when((peer != q) | (core != c))
                def _():
                    push(which, sa.at[phase, c * NQ + peer], ra.at[phase, me], 2 * peer + c, y)

            each(NQ, one, 0)

    def from_core(which, phase, c):
        @pl.when(core == c)
        def _():
            arrive(which, ra.at[phase, pl.ds(0, NQ - 1)])

        @pl.when(core != c)
        def _():
            arrive(which, ra.at[phase, pl.ds(0, NQ)])

    def from_all(which, phase):
        arrive(which, ra.at[phase, pl.ds(0, nt - 1)])

    each(Z, lambda d: push(WZ, wbuf.at[core, xx, z], wbuf.at[core, xx, z], tok_of(xx, lax.rem(z + d, Z)), y))
    a2a(0, A1)

    loads[LF2].wait()
    f2h = f2v[...].astype(bf16)
    f2th, f2tl = split(f2v[...].T)
    band = min(N // 2, 128)

    def row_of(n):
        return 4 * ((n >> 4) & (NQ - 1)) + 2 * (n >> (4 + lgq)) + ((n >> 3) & 1)

    spread = row_of(lax.broadcasted_iota(jnp.int32, (N, R), 0)) == lax.broadcasted_iota(jnp.int32, (N, R), 1)
    spread = jnp.where(spread, 1.0, 0.0).astype(bf16)
    same = ((lax.broadcasted_iota(jnp.int32, (band, N), 0) & 7) == (lax.broadcasted_iota(jnp.int32, (band, N), 1) & 7))

    def picked(r0):
        rows = row_of(lax.broadcasted_iota(jnp.int32, (band, R), 0) + r0)
        return jnp.where(rows == lax.broadcasted_iota(jnp.int32, (band, R), 1), 1.0, 0.0).astype(bf16)

    def build(src, dst):
        def step(b, carry):
            r0 = pl.multiple_of(b * band, band)
            part = mm_nt(mm(picked(r0), src).astype(bf16), spread)
            dst[pl.ds(r0, band), :] = jnp.where(same, part, 0.0).astype(bf16)
            return carry
        lax.fori_loop(0, N // band, step, 0)

    build(f2h, kh)
    build(f2th, kth)

    arrive(WZ, wbuf.at[core, xx, pl.ds(0, Z - 1)])
    def send_wx(e):
        d, part = 1 + lax.rem(e, X - 1), lax.div(e, X - 1)
        push(WX, wbuf.at[core, xx, part], wbuf.at[core, xx, part], tok_of(lax.rem(xx + d, X), z), y)

    each((X - 1) * Z, send_wx, 0)

    from_all(A1, 0)
    mid = ra[0].reshape(N, C)
    sa[1] = mm(kh[...], mid).astype(bf16).reshape(nt, 16, C)
    ra[1, me] = sa[1, me]
    a2a(1, A2 + core)

    arrive(WX, wbuf.at[core, pl.ds(0, X - 1)])
    push(WC, wbuf.at[core], wbuf.at[core], sib, y)
    build(f2tl, ktl)
    mid = ra[0].reshape(N, C).astype(f32)
    for h in range(C // W):
        mid32[h] = mid[:, h * W : (h + 1) * W]
    for c in range(2):
        f1t[c] = f1v[...].reshape(NQ, 2, 8, M)[:, c].reshape(H, M).T.astype(bf16)
    arrive(WC, wbuf.at[other])

    for c in range(2):
        wdn[:, c] = wbuf[c, :, :, 0:16].reshape(NQ, 16, C)
    up_rows = [wbuf[c, :, :, 16:32].astype(f32).reshape(NQ, 1, 16, C) for c in range(2)]
    up_rows = jnp.concatenate(up_rows, axis=1).reshape(N, C)
    for h in range(C // W):
        rows4[h] = up_rows[:, h * W : (h + 1) * W]
    for fq in range(4):
        for h in range(C // W):
            for r in range(4):
                stage[pl.ds(r, nt, stride=4), :] = rows4[h, pl.ds(4 * fq + r, nt, stride=16), :]
            wup[:, fq * C + h * W : fq * C + (h + 1) * W] = stage[...].astype(bf16)

    nb = max(1, NQ // 2)
    tiles = NQ // nb
    TB = nb * 16

    def tokens(ref, c, q0):
        return pair(ref[0, pl.ds(q0, nb), c], ref[1, pl.ds(q0, nb), c]).reshape(TB, C)

    def put(ref, c, q0, value):
        value = value.reshape(nb, 2, 8, C)
        ref[0, pl.ds(q0, nb), c] = value[:, 0]
        ref[1, pl.ds(q0, nb), c] = value[:, 1]

    def places(c, j):
        q0 = pl.multiple_of(j * nb, nb)
        return q0, pl.ds(pl.multiple_of(c * H * 2 + j * TB, TB), TB)

    loads[LOC].wait()
    for c in range(2):
        def pre(j, carry):
            q0, rows = places(c, j)
            c16 = tokens(ocv, c, q0).astype(bf16)
            cot[rows, :] = c16
            dhid[rows, :] = mm_nt(c16, wdn[...].reshape(N, C))
            return carry

        lax.fori_loop(0, tiles, pre, 0)

    for c in range(2):
        from_core(A2 + c, 1, c)

        def mlp(j, carry):
            tile = lax.rem(lax.div(q, nb) + j, tiles)
            q0, rows = places(c, tile)
            mixed = ra[1, pl.ds(c * NQ + q0, nb)].reshape(TB, C).astype(f32)
            inp = tokens(xv, c, q0)
            gate = jax.nn.sigmoid(inp)
            branch = inp + gate * mixed
            put(out_ref, c, q0, branch)
            normed = branch.astype(bf16)
            nrm[rows, :] = normed
            up = mm(normed, wup[...])
            active, slope = gelu_parts(up)
            hid[rows, :] = active.astype(bf16)
            d_up = (dhid[rows, :] * slope).astype(bf16)
            dup[rows, :] = d_up
            d_branch = tokens(ocv, c, q0) + mm_nt(d_up, wup[...])
            sa[2, pl.ds(c * NQ + q0, nb)] = (d_branch * gate).astype(bf16).reshape(nb, 16, C)

            def one(b, inner):
                peer = q0 + lax.rem(q + b, nb)

                @pl.when((peer != q) | (core != c))
                def _():
                    push(A3, sa.at[2, c * NQ + peer], ra.at[2, me], 2 * peer + c, y)

                return inner

            lax.fori_loop(0, nb, one, 0)
            put(gx_ref, c, q0, d_branch * (1.0 + gate * (1.0 - gate) * mixed))
            return carry

        lax.fori_loop(0, tiles, mlp, 0)
    ra[2, me] = sa[2, me]

    from_all(A3, 2)
    grad = ra[2].reshape(N, C)
    sa[3] = (mm(kth[...], grad) + mm(ktl[...], grad)).astype(bf16).reshape(nt, 16, C)
    ra[3, me] = sa[3, me]
    a2a(3, A4 + core)

    gd_part = mm_tn(hid[...], cot[...]).reshape(NQ, 2, 16, C)
    for c in range(2):
        gbuf[c, :, 0:16] = gd_part[:, c]
    for fq in range(4):
        gu_part = mm_tn(nrm[...], dup[:, fq * C : (fq + 1) * C])
        for h in range(C // W):
            stage[...] = gu_part[:, h * W : (h + 1) * W]
            for r in range(4):
                rows4[h, pl.ds(4 * fq + r, nt, stride=16), :] = stage[pl.ds(r, nt, stride=4), :]
    for c in range(2):
        for h in range(C // W):
            gbuf[c, :, 16:32, h * W : (h + 1) * W] = rows4[h].reshape(NQ, 2, 16, W)[:, c]
    sgc[...] = gbuf[other].astype(bf16)
    push(GC, sgc, rgc, sib, y)

    grad = ra[2].reshape(N, C).astype(f32)
    for h in range(C // W):
        rows4[h] = grad[:, h * W : (h + 1) * W]
    total = jnp.zeros((R, R), f32)
    for k in range(8):
        for h in range(C // W):
            total = total + mm_nt(rows4[h, pl.ds(k, R, stride=8), :].astype(bf16),
                                  mid32[h, pl.ds(k, R, stride=8), :].astype(bf16))
    order = row_of(lax.broadcasted_iota(jnp.int32, (R, R), 0) * 8) == lax.broadcasted_iota(jnp.int32, (R, R), 1)
    order = jnp.where(order, 1.0, 0.0).astype(bf16)
    th, tl = split(total)
    th, tl = split(mm(th, order) + mm(tl, order))
    tpart[...] = (mm_tn(order, th) + mm_tn(order, tl)).reshape(2, nt, R)
    push(TC, tpart.at[other], rtc, sib, y)

    for c in range(2):
        def finish(j, carry):
            q0, rows = places(c, j)
            put(out_ref, c, q0, tokens(out_ref, c, q0) + mm(hid[rows, :], wdn[...].reshape(N, C)))
            return carry

        lax.fori_loop(0, tiles, finish, 0)

    def send_py(d):
        peer = lax.rem(y + d, Y)
        push(PY, spy.at[peer], rpy.at[y], t, peer)

    def over_cores():
        arrive(PC, rpc)
        pown[...] = pown[...] + rpc[...].astype(f32)
        spy[...] = pown[...].astype(bf16)
        each(Y, send_py)

    for c in range(2):
        from_core(A4 + c, 3, c)
        d_mid = ra[3, c * NQ : (c + 1) * NQ].astype(f32).reshape(NQ, 2, 8, C)
        one = None
        for i in range(2):
            d_first = (d_mid[:, i] * twc[i, :, c]).reshape(H, C).astype(bf16)
            df[c, i] = d_first
            part = mm_nt(d_first, xb[i]) + mm_nt(d_first, xs[i])
            one = part if one is None else one + part
        one = one.reshape(NQ, 8, M)

        @pl.when(core != c)
        def _():
            for v in range(Y):
                spc[v] = one[:, :, v * LY : (v + 1) * LY].astype(bf16)
            push(PC, spc, rpc, sib, y)

        @pl.when(core == c)
        def _():
            for v in range(Y):
                pown[v] = one[:, :, v * LY : (v + 1) * LY]

        if c == 0:
            @pl.when(core == 0)
            def _():
                over_cores()

    arrive(GC, rgc)
    sgx[...] = (gbuf[core] + rgc[...].astype(f32)).astype(bf16).reshape(X, Z, 32, C)

    def send_gx(d):
        peer = lax.rem(xx + d, X)
        push(GX, sgx.at[peer], rgx.at[xx], tok_of(peer, z), y)

    each(X, send_gx)

    arrive(TC, rtc)
    stz[...] = (tpart[core] + rtc[...]).reshape(Z, nt // Z, R)

    def send_tz(d):
        peer = lax.rem(z + d, Z)
        push(TZ, stz.at[peer], rtz.at[z], tok_of(xx, peer), y)

    each(Z, send_tz)

    @pl.when(core == 1)
    def _():
        over_cores()

    arrive(TZ, rtz.at[pl.ds(0, Z - 1)])
    rtz[z] = stz[z]
    rtx[xx] = rtz[...].sum(axis=0)
    each(X, lambda d: push(TX, rtx.at[xx], rtx.at[xx], tok_of(lax.rem(xx + d, X), z), y))

    arrive(PY, rpy.at[pl.ds(0, Y - 1)])
    rpy[y] = jnp.zeros((NQ, 8, LY), bf16)
    total = pown[y]
    for s in range(Y):
        total = total + rpy[s].astype(f32)
    spq[...] = total.astype(bf16)

    def send_pq(d):
        peer = lax.rem(q + d, NQ)
        push(PQ, spq.at[peer], rpq.at[q], 2 * peer + core, y)

    each(NQ, send_pq)

    for i in range(2):
        d_grid = mm(f1t[0], df[0, i]) + mm(f1t[1], df[1, i])
        gx_ref[i] = gx_ref[i] + d_grid.reshape(NQ, 2, 8, C)

    arrive(GX, rgx.at[pl.ds(0, X - 1)])
    rgx[xx] = jnp.zeros((Z, 32, C), bf16)
    zrows = pl.ds(xx * Z, Z)
    own_gz = gbuf[core, zrows] + rgc[zrows].astype(f32)
    for s in range(X):
        own_gz = own_gz + rgx[s].astype(f32)
    gbuf[core, zrows] = own_gz
    sgz[...] = own_gz.astype(bf16)

    def send_gz(d):
        peer = lax.rem(z + d, Z)
        push(GZ, sgz.at[peer], rgz.at[z], tok_of(xx, peer), y)

    each(Z, send_gz)

    arrive(TX, rtx.at[pl.ds(0, X - 1)])
    rty[y] = rtx[...].sum(axis=0)
    each(Y, lambda d: push(TY, rty.at[y], rty.at[y], t, lax.rem(y + d, Y)))

    arrive(PQ, rpq.at[pl.ds(0, NQ - 1)])
    rpq[q] = spq[q]
    fy[core, y, q] = rpq[...].astype(f32).sum(axis=0).astype(bf16)
    each(NQ, lambda d: push(PQ2, fy.at[core, y, q], fy.at[core, y, q], 2 * lax.rem(q + d, NQ) + core, y))

    arrive(TY, rty.at[pl.ds(0, Y - 1)])
    rt2[core, z] = rty[...].sum(axis=0)
    each(Z, lambda d: push(TZ2, rt2.at[core, z], rt2.at[core, z], tok_of(xx, lax.rem(z + d, Z)), y))

    arrive(GZ, rgz.at[pl.ds(0, Z - 1)])
    rgz[z] = jnp.zeros((32, C), bf16)
    wpack[...] = gbuf[core, xx * Z + z] + rgz[...].astype(f32).sum(axis=0)
    gd_ref[...] = wpack[0:16, :]
    for fq in range(4):
        gu_ref[:, fq * C : (fq + 1) * C] = wpack[16 + 4 * fq : 20 + 4 * fq, :]

    arrive(PQ2, fy.at[core, y, pl.ds(0, NQ - 1)])
    each(Y, lambda d: push(PY2, fy.at[core, y], fy.at[core, y], t, lax.rem(y + d, Y)))
    arrive(TZ2, rt2.at[core, pl.ds(0, Z - 1)])
    push(TC2, rt2.at[core], rt2.at[core], sib, y)
    arrive(PY2, fy.at[core, pl.ds(0, Y - 1)])
    push(PC2, fy.at[core], fy.at[core], sib, y)
    arrive(TC2, rt2.at[other])
    g2_ref[...] = rt2[...].reshape(R, R)
    arrive(PC2, fy.at[other])

    for which, phase in ((A1, 0), (A2 + core, 1), (A3, 2), (A4 + core, 3)):
        sent(which, sa.at[phase, pl.ds(0, nt - 1)])
    sent(WZ, wbuf.at[0, 0, pl.ds(0, Z - 1)])
    sent(WX, wbuf.at[0, pl.ds(0, X - 1)])
    sent(WC, wbuf.at[0])
    sent(GC, rgc)
    sent(GX, sgx.at[pl.ds(0, X - 1)])
    sent(GZ, sgz.at[pl.ds(0, Z - 1)])
    sent(TC, rtc)
    sent(TZ, stz.at[pl.ds(0, Z - 1)])
    sent(TX, rtx.at[pl.ds(0, X - 1)])
    sent(TY, rty.at[pl.ds(0, Y - 1)])
    sent(TZ2, rt2.at[0, pl.ds(0, Z - 1)])
    sent(TC2, rt2.at[0])
    sent(PC, rpc)
    sent(PY, spy.at[pl.ds(0, Y - 1)])
    sent(PQ, spq.at[pl.ds(0, NQ - 1)])
    sent(PQ2, fy.at[0, 0, pl.ds(0, NQ - 1)])
    sent(PY2, fy.at[0, pl.ds(0, Y - 1)])
    sent(PC2, fy.at[0])


def deliver(Y, out_in, gx_in, fy_in, g2_in, gu_in, gd_in,
            out_ref, gx_ref, g1_ref, g2_ref, gu_ref, gd_ref, whole, sem):
    copies = [pltpu.make_async_copy(src, dst, sem.at[n]) for n, (src, dst) in enumerate(
        ((out_in, out_ref), (gx_in, gx_ref), (g2_in, g2_ref), (gu_in, gu_ref), (gd_in, gd_ref)))]
    for copy in copies:
        copy.start()
    NQ = whole.shape[0]
    LY = whole.shape[3] // Y
    for c in range(2):
        for v in range(Y):
            whole[:, c, :, v * LY : (v + 1) * LY] = fy_in[c, v].astype(f32)
    last = pltpu.make_async_copy(whole, g1_ref, sem.at[5])
    last.start()
    for copy in copies:
        copy.wait()
    last.wait()


def local(X, Z, Y, inputs, factor_one, twiddle, factor_two, w_up, w_down, out_cotangent):
    NQ = X * Z
    nt = 2 * NQ
    C = inputs.shape[1]
    M = 8 * nt
    H = 8 * NQ
    N = 16 * nt
    R = 2 * nt
    LY = M // Y
    W = min(C, 128)
    V = pltpu.VMEM
    whole = (2, NQ, 2, 8, C)
    scratch = [
        V(whole, f32), V((M, M), f32), V(whole, f32), V((2, M), f32), V((R, R), f32),
        V((4, 4 * C), bf16), V((16, C), bf16),
        V((4, nt, 16, C), bf16), V((4, nt, 16, C), bf16),
        V((N, N), bf16), V((N, N), bf16), V((N, N), bf16),
        V((2, M, H), bf16), V((2, M, C), bf16), V((2, M, C), bf16), V((2, NQ, 2, 8, 1), f32),
        V((2, X, Z, 32, C), bf16), V((C, 4 * C), bf16), V((NQ, 2, 16, C), bf16),
        V((C, W), f32), V((C // W, N, W), f32),
        V((N, 4 * C), f32), V((N, 4 * C), bf16), V((N, 4 * C), bf16), V((N, C), bf16), V((N, C), bf16),
        V((2, 2, H, C), bf16),
        V((2, NQ, 32, C), f32), V((NQ, 32, C), bf16), V((NQ, 32, C), bf16),
        V((X, Z, 32, C), bf16), V((X, Z, 32, C), bf16), V((Z, 32, C), bf16), V((Z, 32, C), bf16),
        V((C // W, N, W), f32), V((2, nt, R), f32), V((nt, R), f32),
        V((Z, nt // Z, R), f32), V((Z, nt // Z, R), f32), V((X, nt // Z, R), f32), V((Y, nt // Z, R), f32),
        V((2, Z, nt // Z, R), f32),
        V((Y, NQ, 8, LY), f32), V((Y, NQ, 8, LY), bf16), V((Y, NQ, 8, LY), bf16),
        V((Y, NQ, 8, LY), bf16), V((Y, NQ, 8, LY), bf16),
        V((NQ, 8, LY), bf16), V((NQ, 8, LY), bf16),
        V((32, C), f32),
        pltpu.SemaphoreType.DMA((NEX,)), pltpu.SemaphoreType.DMA((NEX,)), pltpu.SemaphoreType.DMA((7,)),
    ]
    small = [((R, R), f32), ((4, 4 * C), f32), ((16, C), f32)]
    held = [(whole, f32), (whole, f32), ((2, Y, NQ, 8, LY), bf16)] + small
    final = [(whole, f32), (whole, f32), ((NQ, 2, 8, M), f32)] + small
    vm = pl.BlockSpec(memory_space=pltpu.VMEM)
    anywhere = pl.BlockSpec(memory_space=pl.ANY)
    results = pl.pallas_call(
        functools.partial(kernel, X, Z, Y),
        out_shape=[pltpu.VMEM(*s) for s in held],
        in_specs=[anywhere] * 7,
        out_specs=[vm] * 6,
        scratch_shapes=scratch,
        compiler_params=pltpu.CompilerParams(
            collective_id=0, has_side_effects=True, vmem_limit_bytes=60 * 1024 * 1024),
        name="monarch",
    )(
        inputs.reshape(whole), factor_one, twiddle, factor_two,
        w_up[0], w_down[0], out_cotangent.reshape(whole),
    )
    out, gx, g1, g2, gu, gd = pl.pallas_call(
        functools.partial(deliver, Y),
        out_shape=[jax.ShapeDtypeStruct(*s) for s in final],
        in_specs=[vm] * 6,
        out_specs=[anywhere] * 6,
        scratch_shapes=[V((NQ, 2, 8, M), f32), pltpu.SemaphoreType.DMA((6,))],
        compiler_params=pltpu.CompilerParams(vmem_limit_bytes=8 * 1024 * 1024),
        name="deliver",
    )(*[pltpu.with_memory_space_constraint(r, pltpu.VMEM) for r in results])
    return (out.reshape(2 * M, C), gx.reshape(2 * M, C), g1.reshape(M, M), g2, gu[None], gd[None])


def solution(mesh):
    nt = mesh.shape["tok"]
    Y = mesh.shape["ch"]
    X = 4 if nt == 64 else 2
    in_specs = (
        P("tok", "ch"),
        P(),
        P("tok", None),
        P(),
        P("ch", "tok", None),
        P("ch", "tok", None),
        P("tok", "ch"),
    )
    out_specs = (
        P("tok", "ch"),
        P("tok", "ch"),
        P(),
        P(),
        P("ch", "tok", None),
        P("ch", "tok", None),
    )
    return jax.shard_map(
        functools.partial(local, X, nt // 2 // X, Y), mesh=mesh, in_specs=in_specs, out_specs=out_specs, check_vma=False)
```
